512 devices in a mesh: dp: 16 (over z_lo, core), seq: 32 (over z_hi, x, y).
Axes of the slice: x: 4, y: 4, z: 16 (z_hi: 2, z_lo: 8; z = z_hi * 8 + z_lo), core: 2. Of those that a mesh axis runs over, the one named last changes fastest.
Arguments:
- tokens: bfloat16 [16, 4096, 1536], P('dp', 'seq'), may hold values from -6 to 6
- upstream: bfloat16 [16, 4096, 1536], P('dp', 'seq'), may hold values from -6 to 6
- conv_value: float32 [3, 1536], replicated, may hold values from -3.5 to 3.5
- conv_gate: float32 [3, 1536], replicated, may hold values from -3.5 to 3.5
- mix_one: bfloat16 [2, 32, 128, 128], P(None, 'seq'), may hold values from -0.375 to 0.375
- mix_two: bfloat16 [2, 128, 32, 32], P(None, 'seq'), may hold values from -0.75 to 0.75
- mix_three: bfloat16 [2, 128, 32, 32], P(None, 'seq'), may hold values from -0.75 to 0.75
- mix_four: bfloat16 [2, 32, 128, 128], P(None, 'seq'), may hold values from -0.375 to 0.375
- filter_log: bfloat16 [128, 32, 1536], P('seq'), may hold values from -2.5 to 2.5
Outputs:
- grad_x: bfloat16 [16, 4096, 1536], P('dp', 'seq')
- grad_conv_value: float32 [3, 1536], replicated
- grad_conv_gate: float32 [3, 1536], replicated
- grad_mix_one: bfloat16 [2, 32, 128, 128], P(None, 'seq')
- grad_mix_two: bfloat16 [2, 128, 32, 32], P(None, 'seq')
- grad_mix_three: bfloat16 [2, 128, 32, 32], P(None, 'seq')
- grad_mix_four: bfloat16 [2, 32, 128, 128], P(None, 'seq')
- grad_filter: bfloat16 [128, 32, 1536], P('seq')
The draws below stay inside these ranges and needn't reach their ends.
All inputs are finite; a program needn't handle non-finite values.
Results may differ from the reference program's by a relative error of at most 0.018.
Values may be sent and summed in bfloat16 or wider, within the bound.
A program may use at most 64 MiB of HBM per device.

```python
import jax
import jax.numpy as jnp
from jax import lax

C = 1536
BLK = 128
LENGTH = 4096
NBLK = 32
SEQS = 16


def strengthened(values, rng, source, target, parts, factor):
    def block_of(dim):
        return (jnp.arange(values.shape[dim]) // (values.shape[dim] // parts)).reshape((-1,) + (1,) * (values.ndim - 1 - dim))

    first = jax.random.permutation(rng, parts)[block_of(target)]
    second = (block_of(target) + parts // 2) % parts
    return jnp.where((block_of(source) == first) | (block_of(source) == second), factor * values, values)


def block_scale(stream_key, shape, split, least, largest):
    def one(axis_at, shards_of):
        draws = jax.random.uniform(jax.random.fold_in(jax.random.fold_in(stream_key, 6), axis_at), (shards_of,), jnp.float32, least / len(split), largest / len(split))
        return jnp.repeat(jnp.exp(draws), shape[axis_at] // shards_of).reshape((-1,) + (1,) * (len(shape) - axis_at - 1))

    factor_of = one(*split[0])
    for cut in split[1:]:
        factor_of = factor_of * one(*cut)
    return factor_of


def centred(rng, dims, scale, reach, cuts=(), kind=jnp.bfloat16):
    values = scale * jax.random.normal(rng, dims, jnp.float32)
    if cuts:
        values = values * block_scale(rng, dims, cuts, -0.22, 0.18)
    return jnp.clip(values, -reach, reach).astype(kind)


def noise_with(rng, shape, deviation, limit, pieces, heavy, dtype=jnp.bfloat16):
    result = deviation * jax.random.normal(rng, shape, jnp.float32)
    if pieces:
        result = result * block_scale(rng, shape, pieces, -0.22, 0.18)
    return jnp.clip(strengthened(result, jax.random.fold_in(rng, 3), *heavy), -limit, limit).astype(dtype)


def setup_inputs(seed: int = 0) -> dict:
    splits = jax.random.split(jax.random.key(seed), 10)
    return {
        "tokens": centred(splits[0], (SEQS, LENGTH, C), 1.0, 6.0, ((0, 16), (1, 32))),
        "upstream": noise_with(splits[1], (SEQS, LENGTH, C), 1.0, 6.0, ((0, 16), (1, 32)), (1, 2, 32, 2.75)),
        "conv_value": centred(splits[2], (3, C), 3 ** -0.5, 3.5, (), jnp.float32),
        "conv_gate": centred(splits[3], (3, C), 3 ** -0.5, 3.5, (), jnp.float32),
        "mix_one": centred(splits[4], (2, NBLK, BLK, BLK), (2 * BLK) ** -0.5, 0.375, ((1, 32),)),
        "mix_two": centred(splits[5], (2, BLK, NBLK, NBLK), (2 * NBLK) ** -0.5, 0.75, ((1, 32),)),
        "mix_three": centred(splits[6], (2, BLK, NBLK, NBLK), (2 * NBLK) ** -0.5, 0.75, ((1, 32),)),
        "mix_four": centred(splits[7], (2, NBLK, BLK, BLK), (2 * BLK) ** -0.5, 0.375, ((1, 32),)),
        "filter_log": centred(splits[8], (BLK, NBLK, C), 0.5, 2.5, ((0, 32),)),
    }


def settle(array):
    return lax.optimization_barrier(array.astype(jnp.bfloat16)).astype(jnp.float32)

def complex_stack(factor, conjugate):
    real_part = factor[0]
    imag_part = factor[1]
    if conjugate:
        return jnp.stack([jnp.stack([real_part, imag_part]), jnp.stack([-imag_part, real_part])])
    return jnp.stack([jnp.stack([real_part, -imag_part]), jnp.stack([imag_part, real_part])])

def shortconv(padded, weights):
    length = padded.shape[0] - 2
    return weights[0] * padded[0:length] + weights[1] * padded[1:length + 1] + weights[2] * padded[2:length + 2]

def conv_grad(grad, padded):
    length = grad.shape[0]
    return jnp.stack([lax.optimization_barrier(jnp.sum(grad * padded[offset:offset + length], axis=0)) for offset in range(3)])

def transpose_conv(grad, weights):
    edged = jnp.pad(grad, ((1, 1), (0, 0)))
    return weights[0] * edged[2:] + weights[1] * edged[1:-1] + weights[2] * edged[:-2]

def one_sequence(seq_tokens, seq_upstream, conv_value, conv_gate, blocks_one, blocks_two, blocks_three, blocks_four, filt):
    padded = jnp.pad(seq_tokens.astype(jnp.float32), ((1, 1), (0, 0)))
    values = settle(shortconv(padded, conv_value))
    gating = settle(shortconv(padded, conv_gate))
    value_blocks = values.reshape(NBLK, BLK, C)
    stacked_two = complex_stack(blocks_two, False)
    stacked_two_conj = complex_stack(blocks_two, True)
    stacked_three = complex_stack(blocks_three, False)
    stacked_three_conj = complex_stack(blocks_three, True)
    signed_four = jnp.stack([blocks_four[0], -blocks_four[1]])
    first = settle(jnp.einsum('pikj,ijc->pikc', blocks_one, value_blocks))
    second = jnp.einsum('pqkmi,qikc->pkmc', stacked_two, first)
    weighted = settle(filt * second)
    third = settle(jnp.einsum('pqknm,qkmc->pknc', stacked_three, weighted))
    mixed_out = jnp.einsum('pnqk,pknc->nqc', signed_four, third).reshape(LENGTH, C)
    upstream_f = seq_upstream.astype(jnp.float32)
    mix_grad = settle(upstream_f * gating)
    gate_grad = upstream_f * mixed_out
    mix_blocks = mix_grad.reshape(NBLK, BLK, C)
    third_grad = settle(jnp.einsum('pnqk,nqc->pknc', signed_four, mix_blocks))
    products = jnp.einsum('nqc,pknc->pnqk', mix_blocks, third)
    grad_four = jnp.stack([products[0], -products[1]])
    weighted_grad = jnp.einsum('pqknm,qknc->pkmc', stacked_three_conj, third_grad)
    products = jnp.einsum('qknc,pkmc->qpknm', third_grad, weighted)
    grad_three = jnp.stack([products[0, 0] + products[1, 1], products[1, 0] - products[0, 1]])
    filter_term = weighted_grad[0] * second[0] + weighted_grad[1] * second[1]
    second_grad = settle(filt * weighted_grad)
    first_grad = settle(jnp.einsum('pqkmi,qkmc->pikc', stacked_two_conj, second_grad))
    products = jnp.einsum('qkmc,pikc->qpkmi', second_grad, first)
    grad_two = jnp.stack([products[0, 0] + products[1, 1], products[1, 0] - products[0, 1]])
    value_grad = jnp.einsum('pikj,pikc->ijc', blocks_one, first_grad).reshape(LENGTH, C)
    grad_one = jnp.einsum('pikc,ijc->pikj', first_grad, value_blocks)
    token_grad = (transpose_conv(value_grad, conv_value) + transpose_conv(gate_grad, conv_gate)).astype(jnp.bfloat16)
    terms = (grad_one, grad_two, grad_three, grad_four, filter_term, conv_grad(value_grad, padded), conv_grad(gate_grad, padded))
    return (token_grad, terms)

def reference(tokens, upstream, conv_value, conv_gate, mix_one, mix_two, mix_three, mix_four, filter_log):
    filt = jnp.exp(filter_log.astype(jnp.float32))
    blocks_one = mix_one.astype(jnp.float32)
    blocks_two = mix_two.astype(jnp.float32)
    blocks_three = mix_three.astype(jnp.float32)
    blocks_four = mix_four.astype(jnp.float32)

    def advance(carry, pair):
        token_grad, terms = one_sequence(pair[0], pair[1], conv_value, conv_gate, blocks_one, blocks_two, blocks_three, blocks_four, filt)
        return (tuple((total + term for total, term in zip(carry, terms))), token_grad)
    initial = (jnp.zeros((2, NBLK, BLK, BLK), jnp.float32), jnp.zeros((2, BLK, NBLK, NBLK), jnp.float32), jnp.zeros((2, BLK, NBLK, NBLK), jnp.float32), jnp.zeros((2, NBLK, BLK, BLK), jnp.float32), jnp.zeros((BLK, NBLK, C), jnp.float32), jnp.zeros((3, C), jnp.float32), jnp.zeros((3, C), jnp.float32))
    totals, grad_x = lax.scan(advance, initial, (tokens, upstream))
    grad_filter = (filt * totals[4]).astype(jnp.bfloat16)
    return (grad_x, totals[5], totals[6], totals[0].astype(jnp.bfloat16), totals[1].astype(jnp.bfloat16), totals[2].astype(jnp.bfloat16), totals[3].astype(jnp.bfloat16), grad_filter)
```

```python
import jax
import jax.numpy as jnp
from jax import lax
from jax.sharding import Mesh, PartitionSpec as P

C = 1536
BLK = 128
SEQ = ("co", "xy")
DP = ("zl", "zh")
ALL = ("zl", "co", "zh", "xy")


def swapped(value):
    other = lax.ppermute(value, ("co", "zh"), [(1, 2), (2, 1)])
    mine = lax.axis_index("co") == lax.axis_index("zh")
    return jnp.where(mine, value, other)


def with_halo(cells, dim, width):
    count = lax.axis_size(SEQ)
    ends = count - 1
    head = lax.slice_in_dim(cells, 0, width, axis=dim)
    tail = lax.slice_in_dim(cells, cells.shape[dim] - width, cells.shape[dim], axis=dim)
    return jnp.concatenate(
        [
            lax.ppermute(tail, SEQ, [(i, i + 1) for i in range(ends)]),
            cells,
            lax.ppermute(head, SEQ, [(i + 1, i) for i in range(ends)]),
        ],
        axis=dim,
    )


def complex_stack(factor, conjugate):
    real_part = factor[0]
    imag_part = factor[1]
    if conjugate:
        return jnp.stack([jnp.stack([real_part, imag_part]), jnp.stack([-imag_part, real_part])])
    return jnp.stack([jnp.stack([real_part, -imag_part]), jnp.stack([imag_part, real_part])])


def shortconv(padded, weights):
    length = padded.shape[0] - 2
    return (
        weights[0] * padded[0:length]
        + weights[1] * padded[1 : length + 1]
        + weights[2] * padded[2 : length + 2]
    )


def edge_apply(edged, weights):
    return weights[0] * edged[2:] + weights[1] * edged[1:-1] + weights[2] * edged[:-2]


def conv_grad(grad, padded):
    length = grad.shape[0]
    return jnp.stack(
        [jnp.sum(grad * padded[offset : offset + length], axis=0) for offset in range(3)]
    )


def shards(
    tokens, upstream, conv_value, conv_gate, mix_one, mix_two, mix_three, mix_four, filter_log
):
    tokens = swapped(tokens)
    upstream = swapped(upstream)
    mix_one = swapped(mix_one)
    mix_two = swapped(mix_two)
    mix_three = swapped(mix_three)
    mix_four = swapped(mix_four)
    filter_log = swapped(filter_log)
    local_tokens = tokens[0]
    length = local_tokens.shape[0]
    blocks_here = length // BLK
    stacked_two = complex_stack(mix_two, False)
    stacked_two_conj = complex_stack(mix_two, True)
    stacked_three = complex_stack(mix_three, False)
    stacked_three_conj = complex_stack(mix_three, True)
    signed_four = jnp.stack([mix_four[0], -mix_four[1]])
    padded = with_halo(local_tokens, 0, 1).astype(jnp.float32)
    values = shortconv(padded, conv_value).astype(jnp.bfloat16)
    gating = shortconv(padded, conv_gate).astype(jnp.bfloat16)
    value_blocks = values.reshape(blocks_here, BLK, C)
    first = jnp.einsum(
        "pikj,ijc->pikc", mix_one, value_blocks, preferred_element_type=jnp.float32
    ).astype(jnp.bfloat16)
    first_freq = lax.all_to_all(first, SEQ, split_axis=2, concat_axis=1, tiled=True)
    second = jnp.einsum(
        "pqkmi,qikc->pkmc", stacked_two, first_freq, preferred_element_type=jnp.float32
    )
    filt = jnp.exp(filter_log.astype(jnp.float32))
    weighted = (filt * second).astype(jnp.bfloat16)
    third = jnp.einsum(
        "pqknm,qkmc->pknc", stacked_three, weighted, preferred_element_type=jnp.float32
    ).astype(jnp.bfloat16)
    third_time = lax.all_to_all(third, SEQ, split_axis=2, concat_axis=1, tiled=True)
    mixed_out = jnp.einsum(
        "pnqk,pknc->nqc", signed_four, third_time, preferred_element_type=jnp.float32
    ).reshape(length, C)
    upstream_f = upstream[0].astype(jnp.float32)
    mix_grad = (upstream_f * gating.astype(jnp.float32)).astype(jnp.bfloat16)
    gate_grad = upstream_f * mixed_out
    mix_blocks = mix_grad.reshape(blocks_here, BLK, C)
    third_grad = jnp.einsum(
        "pnqk,nqc->pknc", signed_four, mix_blocks, preferred_element_type=jnp.float32
    ).astype(jnp.bfloat16)
    products = jnp.einsum(
        "nqc,pknc->pnqk", mix_blocks, third_time, preferred_element_type=jnp.float32
    )
    grad_four = jnp.stack([products[0], -products[1]])
    third_grad_freq = lax.all_to_all(third_grad, SEQ, split_axis=1, concat_axis=2, tiled=True)
    weighted_grad = jnp.einsum(
        "pqknm,qknc->pkmc", stacked_three_conj, third_grad_freq, preferred_element_type=jnp.float32
    )
    products = jnp.einsum(
        "qknc,pkmc->qpknm", third_grad_freq, weighted, preferred_element_type=jnp.float32
    )
    grad_three = jnp.stack([products[0, 0] + products[1, 1], products[1, 0] - products[0, 1]])
    filter_term = weighted_grad[0] * second[0] + weighted_grad[1] * second[1]
    filter_part = lax.psum_scatter(filter_term, DP, scatter_dimension=1, tiled=True)
    share = filter_part.shape[1]
    filt_share = lax.dynamic_slice_in_dim(filt, lax.axis_index(DP) * share, share, 1)
    finished = (filt_share * filter_part).astype(jnp.bfloat16)
    grad_filter = lax.all_gather(finished, DP, axis=1, tiled=True)
    second_grad = (filt * weighted_grad).astype(jnp.bfloat16)
    first_grad = jnp.einsum(
        "pqkmi,qkmc->pikc", stacked_two_conj, second_grad, preferred_element_type=jnp.float32
    ).astype(jnp.bfloat16)
    products = jnp.einsum(
        "qkmc,pikc->qpkmi", second_grad, first_freq, preferred_element_type=jnp.float32
    )
    grad_two = jnp.stack([products[0, 0] + products[1, 1], products[1, 0] - products[0, 1]])
    first_grad_time = lax.all_to_all(first_grad, SEQ, split_axis=1, concat_axis=2, tiled=True)
    value_grad = jnp.einsum(
        "pikj,pikc->ijc", mix_one, first_grad_time, preferred_element_type=jnp.float32
    ).reshape(length, C)
    grad_one = jnp.einsum(
        "pikc,ijc->pikj", first_grad_time, value_blocks, preferred_element_type=jnp.float32
    )
    edged = with_halo(jnp.stack([value_grad, gate_grad]), 1, 1)
    token_grad = (edge_apply(edged[0], conv_value) + edge_apply(edged[1], conv_gate)).astype(
        jnp.bfloat16
    )
    conv_value_grad, conv_gate_grad = lax.psum(
        (conv_grad(value_grad, padded), conv_grad(gate_grad, padded)), ALL
    )
    grads = lax.psum((grad_one, grad_two, grad_three, grad_four), DP)
    grads = [grad.astype(jnp.bfloat16) for grad in grads] + [grad_filter]
    mine = lax.axis_index("co") == lax.axis_index("zh")
    grads = [
        jnp.where(mine, grad, lax.ppermute(grad, "co", [(0, 1), (1, 0)])) for grad in grads
    ]
    return (
        swapped(token_grad[None]),
        conv_value_grad,
        conv_gate_grad,
        *grads,
    )


def solution(mesh):
    inner = Mesh(mesh.devices.reshape(8, 2, 2, 16), ALL)
    rows = ("zl", "co")
    cols = ("zh", "xy")
    block = P(None, cols, None, None)
    return jax.shard_map(
        shards,
        mesh=inner,
        in_specs=(
            P(rows, cols, None),
            P(rows, cols, None),
            P(),
            P(),
            block,
            block,
            block,
            block,
            P(cols, None, None),
        ),
        out_specs=(
            P(rows, cols, None),
            P(),
            P(),
            block,
            block,
            block,
            block,
            P(cols, None, None),
        ),
        check_vma=False,
    )
```

```python
import jax
import jax.numpy as jnp
from jax import lax
from jax.experimental import pallas as pl
from jax.experimental.pallas import tpu as pltpu
from jax.sharding import Mesh, PartitionSpec as P

C = 1536
ALL = ("zl", "co", "zh", "xy")
MESH = pl.DeviceIdType.MESH
F32 = jnp.float32
BF16 = jnp.bfloat16
CHUNKS = 2
W = C // CHUNKS
TILE = 256
TILES = W // TILE


def iota(shape, dim):
    return lax.broadcasted_iota(jnp.int32, shape, dim)


def dot(a, b):
    return lax.dot_general(a, b, (((1,), (0,)), ((), ())), preferred_element_type=F32)


def dot_nt(a, b):
    return lax.dot_general(a, b, (((1,), (1,)), ((), ())), preferred_element_type=F32)


def await_bytes(ref, sem):
    pltpu.make_async_copy(ref, ref, sem).wait()


def kernel(
    tok,
    ups,
    flog,
    fact,
    cval,
    cgate,
    gx_out,
    gf_out,
    gg_out,
    cv_out,
    ts,
    us,
    fl,
    fa,
    halo,
    w14,
    w14t,
    bmat,
    bmatt,
    filt,
    ymat,
    xs,
    xr,
    vmat,
    zs,
    zr,
    ft,
    gbs,
    gws,
    dbm,
    dwm,
    vgs,
    ggs,
    es,
    er,
    gxs,
    rf,
    rb,
    rw,
    fin,
    gbf,
    gwf,
    cp,
    rc,
    cs,
    rz,
    ct,
    s_in,
    r_edge,
    r_t,
    r_u,
    s_fa,
    r_fa,
    s_halo,
    r_halo,
    s_x,
    r_x,
    s_z,
    r_z,
    s_e,
    r_e,
    s_out,
    r_out,
    s_rf,
    r_rf,
    s_rb,
    r_rb,
    s_rw,
    r_rw,
    s_gf,
    r_gf,
    s_gb,
    r_gb,
    s_gw,
    r_gw,
    s_sib,
    s_c1,
    r_c1,
    s_c2,
    r_c2,
    s_c3,
    r_c3,
):
    zl, co, zh, xy = (lax.axis_index(name) for name in ALL)
    me = co * 16 + xy
    z = zh * 8 + zl
    native = co == zh
    partner = (zl, 1 - co, 1 - zh, xy)
    sibling = (zl, 1 - co, zh, xy)

    def plane(j):
        return (zl, j // 16, zh, lax.rem(j, 16))

    def ring(k):
        return (lax.rem(k, 8), co, k // 8, xy)

    def remote(src, dst, ss, rs, dev):
        return pltpu.make_async_remote_copy(
            src_ref=src, dst_ref=dst, send_sem=ss, recv_sem=rs, device_id=dev, device_id_type=MESH
        )

    up = lax.rem(z + 1, 16)
    down = lax.rem(z + 15, 16)

    barrier = pltpu.get_barrier_semaphore()

    def greet_plane(i, carry):
        pl.semaphore_signal(
            barrier, inc=1, device_id=plane(lax.rem(me + i, 32)), device_id_type=MESH
        )
        return carry

    def greet_ring(i, carry):
        pl.semaphore_signal(
            barrier, inc=1, device_id=ring(lax.rem(z + i, 16)), device_id_type=MESH
        )
        return carry

    pl.semaphore_signal(barrier, inc=1, device_id=partner, device_id_type=MESH)
    lax.fori_loop(1, 16, greet_ring, 0)
    lax.fori_loop(1, 32, greet_plane, 0)
    pl.semaphore_wait(barrier, 47)

    def role_copies():
        out = []
        for lo, hi in ((0, 16), (112, 128)):
            part = pl.ds(lo, hi - lo)
            out.append((tok.at[part], ts.at[part], r_edge))
        for n in range(CHUNKS):
            cols = pl.ds(n * W, W)
            mid = pl.ds(16, 96)
            out.append((tok.at[mid, cols], ts.at[mid, cols], r_t.at[n]))
            out.append((ups.at[:, cols], us.at[:, cols], r_u.at[n]))
        return out

    @pl.when(native)
    def _():
        pltpu.make_async_copy(fact, fa, r_fa.at[0]).start()
        pltpu.make_async_copy(flog, fl, r_fa.at[1]).start()
        for src, dst, sem in role_copies():
            pltpu.make_async_copy(src, dst, sem).start()

        @pl.when(zl == 0)
        def _():
            remote(fact, fa, s_fa.at[0], r_fa.at[0], ring(down)).start()
            remote(flog, fl, s_fa.at[1], r_fa.at[1], ring(down)).start()

        @pl.when(zl == 7)
        def _():
            remote(fact, fa, s_fa.at[0], r_fa.at[0], ring(up)).start()
            remote(flog, fl, s_fa.at[1], r_fa.at[1], ring(up)).start()

    @pl.when(jnp.logical_not(native))
    def _():
        for i, (src, dst, sem) in enumerate(role_copies()):
            remote(src, dst, s_in.at[i], sem, partner).start()

    def forward(src, slot):
        @pl.when(jnp.logical_not(native) & (zl < 3))
        def _():
            remote(src, src, s_fa.at[slot], r_fa.at[slot], ring(up)).start()

        @pl.when(jnp.logical_not(native) & (zl > 4))
        def _():
            remote(src, src, s_fa.at[slot], r_fa.at[slot], ring(down)).start()

    await_bytes(ts.at[pl.ds(0, 32)], r_edge)

    @pl.when(me > 0)
    def _():
        remote(ts.at[pl.ds(0, 16)], halo.at[1], s_halo.at[0], r_halo.at[1], plane(me - 1)).start()

    @pl.when(me < 31)
    def _():
        remote(
            ts.at[pl.ds(112, 16)], halo.at[0], s_halo.at[1], r_halo.at[0], plane(me + 1)
        ).start()

    await_bytes(fa, r_fa.at[0])
    forward(fa, 0)
    wc = fa[pl.ds(0, 512), :]
    first_row = lax.rem(iota((512, 128), 0) // 8, 2) == 0
    zero = jnp.zeros_like(wc)
    w14[:, pl.ds(0, 128)] = jnp.where(first_row, wc, zero)
    w14[:, pl.ds(128, 128)] = jnp.where(first_row, zero, wc)
    eye = (iota((128, 128), 0) == iota((128, 128), 1)).astype(BF16)
    wct = dot_nt(eye, wc)
    first_col = lax.rem(iota((128, 512), 1) // 8, 2) == 0
    w14t[pl.ds(0, 128), :] = jnp.where(first_col, wct, 0.0).astype(BF16)
    w14t[pl.ds(128, 128), :] = jnp.where(first_col, 0.0, wct).astype(BF16)

    def block_mask(rows, cols):
        return (lax.rem(rows // 8, 2) == cols // 256) & (
            lax.rem(rows // 2, 4) == lax.rem(cols // 32, 4)
        )

    dc = fa[pl.ds(512, 512), :]
    for n in range(4):
        part = pl.ds(n * 128, 128)
        s = iota((128, 128), 1) + n * 128
        l = iota((128, 128), 0)
        spread = (l == lax.rem(s // 128, 2) * 32 + lax.rem(s, 32)).astype(BF16)
        wide = dot(dc, spread)
        keep = block_mask(iota((512, 128), 0), iota((512, 128), 1) + n * 128)
        bmat[:, part] = jnp.where(keep, wide, 0.0).astype(BF16)
        s = iota((128, 128), 0) + n * 128
        l = iota((128, 128), 1)
        spread = (l == lax.rem(s // 128, 2) * 32 + lax.rem(s, 32)).astype(BF16)
        tall = dot_nt(spread, dc)
        keep = block_mask(iota((128, 512), 1), iota((128, 512), 0) + n * 128)
        bmatt[part, :] = jnp.where(keep, tall, 0.0).astype(BF16)

    dbm[...] = jnp.zeros_like(dbm)
    dwm[...] = jnp.zeros_like(dwm)

    @pl.when(me == 0)
    def _():
        halo[0] = jnp.zeros((16, C), BF16)

    @pl.when(me == 31)
    def _():
        halo[1] = jnp.zeros((16, C), BF16)

    @pl.when(me > 0)
    def _():
        await_bytes(halo.at[0], r_halo.at[0])

    @pl.when(me < 31)
    def _():
        await_bytes(halo.at[1], r_halo.at[1])

    rows = iota((128, TILE), 0)

    def shifted(x, before, after):
        prev = jnp.where(rows == 0, before, pltpu.roll(x, 1, axis=0))
        nxt = jnp.where(rows == 127, after, pltpu.roll(x, 127, axis=0))
        return prev, nxt

    def token_windows(cols):
        x = ts[:, cols].astype(F32)
        before = halo[0, :, cols].astype(F32)[15:16]
        after = halo[1, :, cols].astype(F32)[0:1]
        prev, nxt = shifted(x, before, after)
        return prev, x, nxt

    def tile_cols(n, i):
        return pl.ds(pl.multiple_of(n * W + i * TILE, TILE), TILE)

    def all_to_all(src, dst, ss, rs, n):
        cols = pl.ds(n * W, W)

        def send(i, carry):
            j = lax.rem(me + i, 32)
            remote(src.at[j, :, cols], dst.at[me, :, cols], ss.at[n], rs.at[n], plane(j)).start()
            return carry

        lax.fori_loop(1, 32, send, 0)
        pltpu.make_async_copy(src.at[me, :, cols], dst.at[me, :, cols], rs.at[n]).start()

    def phase_one(n):
        part = pl.ds(n * W, W)
        await_bytes(ts.at[pl.ds(16, 96), part], r_t.at[n])
        await_bytes(us.at[:, part], r_u.at[n])

        def tile(i, carry):
            cols = tile_cols(n, i)
            prev, x, nxt = token_windows(cols)
            cv = cval[:, cols]
            cg = cgate[:, cols]
            values = cv[0:1] * prev + cv[1:2] * x + cv[2:3] * nxt
            gating = (cg[0:1] * prev + cg[1:2] * x + cg[2:3] * nxt).astype(BF16).astype(F32)
            mix = us[:, cols].astype(F32) * gating
            ymat[pl.ds(0, 128), cols] = values.astype(BF16)
            ymat[pl.ds(128, 128), cols] = mix.astype(BF16)
            y = ymat[:, cols]
            xs[:, :, cols] = dot(w14[...], y).astype(BF16).reshape(32, 16, TILE)
            return carry

        lax.fori_loop(0, TILES, tile, 0)
        all_to_all(xs, xr, s_x, r_x, n)

    def reduce_send(src, size, dst, ss, rs):
        def send(k, carry):
            piece = src(pl.ds(pl.multiple_of(k * size, size), size))
            mine = native & (k == zl)

            @pl.when(mine)
            def _():
                pltpu.make_async_copy(piece, dst, rs).start()

            @pl.when(jnp.logical_not(mine))
            def _():
                remote(piece, dst, ss, rs, (k, co, co, xy)).start()

            return carry

        lax.fori_loop(0, 8, send, 0)

    def gather_send(src, dst, ss, rs):
        pltpu.make_async_copy(src, dst, rs).start()

        def send(i, carry):
            k = lax.rem(zl + i, 8)
            remote(src, dst, ss, rs, (k, co, co, xy)).start()
            return carry

        lax.fori_loop(1, 8, send, 0)

    def phase_two(n):
        part = pl.ds(n * W, W)
        await_bytes(xr.at[:, :, part], r_x.at[n])

        def tile(i, carry):
            cols = tile_cols(n, i)
            x = xr[:, :, cols].reshape(512, TILE)
            both = dot(bmatt[...], x)
            f = jnp.exp(fl[:, cols].astype(F32))
            filt[:, cols] = f
            sr = both[0:128]
            si = both[128:256]
            gr = both[256:384]
            gi = both[384:512]
            ft[:, cols] = (gr * sr + gi * si).astype(BF16)
            vmat[pl.ds(0, 128), cols] = (f * gr).astype(BF16)
            vmat[pl.ds(128, 128), cols] = (f * gi).astype(BF16)
            vmat[pl.ds(256, 128), cols] = (f * sr).astype(BF16)
            vmat[pl.ds(384, 128), cols] = (f * si).astype(BF16)
            v = vmat[:, cols]
            zs[:, :, cols] = dot(bmat[...], v).astype(BF16).reshape(32, 16, TILE)
            return carry

        lax.fori_loop(0, TILES, tile, 0)
        all_to_all(zs, zr, s_z, r_z, n)
        reduce_send(lambda piece: ft.at[piece, part], 16, rf.at[z, :, part], s_rf.at[n], r_rf.at[n])

        def tile_grad(i, carry):
            cols = tile_cols(n, i)
            dbm[...] += dot_nt(xr[:, :, cols].reshape(512, TILE), vmat[:, cols])
            return carry

        lax.fori_loop(0, TILES, tile_grad, 0)

    def phase_three(n):
        part = pl.ds(n * W, W)
        await_bytes(zr.at[:, :, part], r_z.at[n])

        def tile(i, carry):
            cols = tile_cols(n, i)
            zt = zr[:, :, cols].reshape(512, TILE)
            both = dot(w14t[...], zt)
            vg = both[0:128]
            gg = us[:, cols].astype(F32) * both[128:256]
            vgs[:, cols] = vg
            ggs[:, cols] = gg
            cv = cval[:, cols]
            cg = cgate[:, cols]
            es[0, :, cols] = jnp.broadcast_to(cv[0:1] * vg[0:1] + cg[0:1] * gg[0:1], (8, TILE))
            es[1, :, cols] = jnp.broadcast_to(
                cv[2:3] * vg[127:128] + cg[2:3] * gg[127:128], (8, TILE)
            )
            return carry

        lax.fori_loop(0, TILES, tile, 0)

        @pl.when(me > 0)
        def _():
            remote(
                es.at[0, :, part], er.at[1, :, part], s_e.at[n, 0], r_e.at[n, 1], plane(me - 1)
            ).start()

        @pl.when(me < 31)
        def _():
            remote(
                es.at[1, :, part], er.at[0, :, part], s_e.at[n, 1], r_e.at[n, 0], plane(me + 1)
            ).start()

        def tile_grad(i, carry):
            cols = tile_cols(n, i)
            prev, x, nxt = token_windows(cols)
            row = lax.broadcasted_iota(jnp.int32, (8, TILE), 0)
            total = jnp.zeros((8, TILE), F32)
            for at, grad in ((0, vgs[:, cols]), (3, ggs[:, cols])):
                for o, window in enumerate((prev, x, nxt)):
                    total += jnp.where(
                        row == at + o, jnp.sum(grad * window, axis=0, keepdims=True), 0.0
                    )
            for k in range(TILE // 128):
                cp[(n * W + i * TILE) // 128 + k] = total[:, k * 128 : (k + 1) * 128]
            dwm[...] += dot_nt(zr[:, :, cols].reshape(512, TILE), ymat[:, cols])
            return carry

        lax.fori_loop(0, TILES, tile_grad, 0)

    def phase_out(n):
        part = pl.ds(n * W, W)

        @pl.when(me == 0)
        def _():
            er[0, :, part] = jnp.zeros((8, W), F32)

        @pl.when(me == 31)
        def _():
            er[1, :, part] = jnp.zeros((8, W), F32)

        @pl.when(me > 0)
        def _():
            await_bytes(er.at[0, :, part], r_e.at[n, 0])

        @pl.when(me < 31)
        def _():
            await_bytes(er.at[1, :, part], r_e.at[n, 1])

        def tile(i, carry):
            cols = tile_cols(n, i)
            cv = cval[:, cols]
            cg = cgate[:, cols]
            vg = vgs[:, cols]
            gg = ggs[:, cols]
            ahead = cv[0:1] * vg + cg[0:1] * gg
            behind = cv[2:3] * vg + cg[2:3] * gg
            here = cv[1:2] * vg + cg[1:2] * gg
            first = er[0, :, cols][0:1]
            last = er[1, :, cols][0:1]
            down_rows = jnp.where(rows == 0, first, pltpu.roll(behind, 1, axis=0))
            up_rows = jnp.where(rows == 127, last, pltpu.roll(ahead, 127, axis=0))
            gxs[:, cols] = (up_rows + here + down_rows).astype(BF16)
            return carry

        lax.fori_loop(0, TILES, tile, 0)

        @pl.when(native)
        def _():
            pltpu.make_async_copy(gxs.at[:, part], gx_out.at[:, part], r_out.at[n]).start()

        @pl.when(jnp.logical_not(native))
        def _():
            remote(
                gxs.at[:, part], gx_out.at[:, part], s_out.at[n], r_out.at[n], partner
            ).start()

    def filter_finish(n):
        part = pl.ds(n * W, W)

        @pl.when(native)
        def _():
            await_bytes(rf.at[:, :, part], r_rf.at[n])

            def tile(i, carry):
                cols = tile_cols(n, i)
                total = rf[0, :, cols].astype(F32)
                for k in range(1, 16):
                    total += rf[k, :, cols].astype(F32)
                share = filt[pl.ds(pl.multiple_of(zl * 16, 16), 16), cols]
                fin[:, cols] = (share * total).astype(BF16)
                return carry

            lax.fori_loop(0, TILES, tile, 0)
            mine = pl.ds(pl.multiple_of(zl * 16, 16), 16)
            gather_send(fin.at[:, part], gf_out.at[mine, part], s_gf.at[n], r_gf.at[n])

    phase_one(0)
    await_bytes(fl, r_fa.at[1])
    forward(fl, 1)
    for n in range(CHUNKS):
        phase_two(n)
        if n + 1 < CHUNKS:
            phase_one(n + 1)

    keep_rows = iota((512, 128), 0)
    packed = [jnp.zeros((512, 128), F32), jnp.zeros((512, 128), F32)]
    for n in range(4):
        part = pl.ds(n * 128, 128)
        keep = block_mask(keep_rows, iota((512, 128), 1) + n * 128)
        q = jnp.where(keep, dbm[:, part], 0.0).astype(BF16)
        s = iota((128, 128), 0) + n * 128
        l = iota((128, 128), 1)
        same = (s // 256 == l // 64) & (lax.rem(s, 32) == lax.rem(l, 32))
        part_of = lax.rem(s // 128, 2)
        imag = lax.rem(l // 32, 2)
        for p in range(2):
            hit = same & (part_of == (imag if p == 0 else 1 - imag))
            minus = (imag == 1) & (l // 64 != p)
            sel = jnp.where(hit, jnp.where(minus, -1.0, 1.0), 0.0).astype(BF16)
            packed[p] = packed[p] + dot(q, sel)
    gb = jnp.zeros((128, 128), F32)
    a = iota((128, 512), 0)
    r = iota((128, 512), 1)
    for p in range(2):
        pick = (r // 16 == a // 4) & (lax.rem(r // 2, 4) == lax.rem(a, 4)) & (lax.rem(r, 2) == p)
        gb = gb + dot(pick.astype(BF16), packed[p].astype(BF16))
    gbs[...] = gb.astype(BF16)
    reduce_send(lambda piece: gbs.at[piece], 16, rb.at[z], s_rb, r_rb)

    for n in range(CHUNKS):
        phase_three(n)
        phase_out(n)
        filter_finish(n)

    t_first = lax.rem(iota((512, 128), 0) // 8, 2) == 0
    gws[...] = jnp.where(t_first, dwm[:, pl.ds(0, 128)], dwm[:, pl.ds(128, 128)]).astype(BF16)
    reduce_send(lambda piece: gws.at[piece], 64, rw.at[z], s_rw, r_rw)

    def tap_send(k, carry):
        @pl.when(k == me)
        def _():
            pltpu.make_async_copy(cp.at[k], rc.at[me], r_c1).start()

        @pl.when(k != me)
        def _():
            remote(cp.at[k], rc.at[me], s_c1, r_c1, plane(k)).start()

        return carry

    lax.fori_loop(0, 12, tap_send, 0)

    @pl.when(native)
    def _():
        await_bytes(rb, r_rb)
        total = rb[0].astype(F32)
        for k in range(1, 16):
            total += rb[k].astype(F32)
        gbf[...] = total.astype(BF16)
        row = pl.ds(pl.multiple_of(512 + zl * 16, 16), 16)
        gather_send(gbf, gg_out.at[row], s_gb, r_gb)

    owner = me < 12

    @pl.when(owner)
    def _():
        await_bytes(rc, r_c1)
        cs[...] = jnp.sum(rc[...], axis=0)
        pltpu.make_async_copy(cs, rz.at[z], r_c2).start()

        def send(i, carry):
            remote(cs, rz.at[z], s_c2, r_c2, ring(lax.rem(z + i, 16))).start()
            return carry

        lax.fori_loop(1, 16, send, 0)

    @pl.when(native)
    def _():
        await_bytes(rw, r_rw)
        total = rw[0].astype(F32)
        for k in range(1, 16):
            total += rw[k].astype(F32)
        gwf[...] = total.astype(BF16)
        row = pl.ds(pl.multiple_of(zl * 64, 64), 64)
        gather_send(gwf, gg_out.at[row], s_gw, r_gw)

    @pl.when(owner)
    def _():
        await_bytes(rz, r_c2)
        ct[...] = jnp.sum(rz[...], axis=0)
        pltpu.make_async_copy(ct, cv_out.at[me], r_c3).start()

        def send(i, carry):
            remote(ct, cv_out.at[me], s_c3, r_c3, plane(lax.rem(me + i, 32))).start()
            return carry

        lax.fori_loop(1, 32, send, 0)

    low = pl.ds(0, 512)
    high = pl.ds(512, 128)

    @pl.when(native)
    def _():
        for n in range(CHUNKS):
            part = pl.ds(n * W, W)
            await_bytes(gf_out.at[:, part], r_gf.at[n])
            remote(
                gf_out.at[:, part], gf_out.at[:, part], s_sib.at[n], r_gf.at[n], sibling
            ).start()
        await_bytes(gg_out.at[high], r_gb)
        remote(gg_out.at[high], gg_out.at[high], s_sib.at[CHUNKS], r_gb, sibling).start()
        await_bytes(gg_out.at[low], r_gw)
        remote(gg_out.at[low], gg_out.at[low], s_sib.at[CHUNKS + 1], r_gw, sibling).start()

    @pl.when(jnp.logical_not(native))
    def _():
        for n in range(CHUNKS):
            await_bytes(gf_out.at[:, pl.ds(n * W, W)], r_gf.at[n])
        await_bytes(gg_out.at[high], r_gb)
        await_bytes(gg_out.at[low], r_gw)

    await_bytes(cv_out, r_c3)
    for n in range(CHUNKS):
        await_bytes(gx_out.at[:, pl.ds(n * W, W)], r_out.at[n])

    @pl.when(jnp.logical_not(native))
    def _():
        for i, (src, dst, sem) in enumerate(role_copies()):
            await_bytes(dst, s_in.at[i])
        for n in range(CHUNKS):
            await_bytes(gxs.at[:, pl.ds(n * W, W)], s_out.at[n])

        @pl.when((zl < 3) | (zl > 4))
        def _():
            await_bytes(fa, s_fa.at[0])
            await_bytes(fl, s_fa.at[1])

    @pl.when(me > 0)
    def _():
        await_bytes(halo.at[1], s_halo.at[0])
        for n in range(CHUNKS):
            await_bytes(es.at[0, :, pl.ds(n * W, W)], s_e.at[n, 0])

    @pl.when(me < 31)
    def _():
        await_bytes(halo.at[0], s_halo.at[1])
        for n in range(CHUNKS):
            await_bytes(es.at[1, :, pl.ds(n * W, W)], s_e.at[n, 1])

    for n in range(CHUNKS):
        part = pl.ds(n * W, W)
        await_bytes(xs.at[pl.ds(0, 31), :, part], s_x.at[n])
        await_bytes(zs.at[pl.ds(0, 31), :, part], s_z.at[n])

    @pl.when(native)
    def _():
        @pl.when((zl == 0) | (zl == 7))
        def _():
            await_bytes(fa, s_fa.at[0])
            await_bytes(fl, s_fa.at[1])

        for n in range(CHUNKS):
            part = pl.ds(n * W, W)
            await_bytes(ft.at[pl.ds(0, 112), part], s_rf.at[n])
            await_bytes(gf_out.at[pl.ds(0, 112), part], s_gf.at[n])
            await_bytes(gf_out.at[:, part], s_sib.at[n])
        await_bytes(gbs.at[pl.ds(0, 112)], s_rb)
        await_bytes(gws.at[pl.ds(0, 448)], s_rw)
        await_bytes(gbs.at[pl.ds(0, 112)], s_gb)
        await_bytes(gws.at[pl.ds(0, 448)], s_gw)
        await_bytes(gg_out.at[high], s_sib.at[CHUNKS])
        await_bytes(gg_out.at[low], s_sib.at[CHUNKS + 1])

    @pl.when(jnp.logical_not(native))
    def _():
        for n in range(CHUNKS):
            await_bytes(ft.at[:, pl.ds(n * W, W)], s_rf.at[n])
        await_bytes(gbs, s_rb)
        await_bytes(gws, s_rw)

    @pl.when(owner)
    def _():
        await_bytes(cp.at[pl.ds(0, 11)], s_c1)
        await_bytes(rz.at[pl.ds(0, 15)], s_c2)
        await_bytes(rc.at[pl.ds(0, 31)], s_c3)

    @pl.when(jnp.logical_not(owner))
    def _():
        await_bytes(cp, s_c1)


def mixer(tok, ups, flog, fact, cval, cgate):
    vmem = pl.BlockSpec(memory_space=pltpu.VMEM)
    hbm = pl.BlockSpec(memory_space=pl.ANY)
    dma = pltpu.SemaphoreType.DMA
    scratch = [
        ((128, C), BF16),
        ((128, C), BF16),
        ((128, C), BF16),
        ((1024, 128), BF16),
        ((2, 16, C), BF16),
        ((512, 256), BF16),
        ((256, 512), BF16),
        ((512, 512), BF16),
        ((512, 512), BF16),
        ((128, C), F32),
        ((256, C), BF16),
        ((32, 16, C), BF16),
        ((32, 16, C), BF16),
        ((512, C), BF16),
        ((32, 16, C), BF16),
        ((32, 16, C), BF16),
        ((128, C), BF16),
        ((128, 128), BF16),
        ((512, 128), BF16),
        ((512, 512), F32),
        ((512, 256), F32),
        ((128, C), F32),
        ((128, C), F32),
        ((2, 8, C), F32),
        ((2, 8, C), F32),
        ((128, C), BF16),
        ((16, 16, C), BF16),
        ((16, 16, 128), BF16),
        ((16, 64, 128), BF16),
        ((16, C), BF16),
        ((16, 128), BF16),
        ((64, 128), BF16),
        ((12, 8, 128), F32),
        ((32, 8, 128), F32),
        ((8, 128), F32),
        ((16, 8, 128), F32),
        ((8, 128), F32),
    ]
    n = CHUNKS
    sems = [
        (2 + 2 * n,),
        (),
        (n,),
        (n,),
        (2,),
        (2,),
        (2,),
        (2,),
        (n,),
        (n,),
        (n,),
        (n,),
        (n, 2),
        (n, 2),
        (n,),
        (n,),
        (n,),
        (n,),
        (),
        (),
        (),
        (),
        (n,),
        (n,),
        (),
        (),
        (),
        (),
        (n + 2,),
        (),
        (),
        (),
        (),
        (),
        (),
    ]
    return pl.pallas_call(
        kernel,
        out_shape=(
            jax.ShapeDtypeStruct((128, C), BF16),
            jax.ShapeDtypeStruct((128, C), BF16),
            jax.ShapeDtypeStruct((640, 128), BF16),
            jax.ShapeDtypeStruct((12, 8, 128), F32),
        ),
        in_specs=[hbm, hbm, hbm, hbm, vmem, vmem],
        out_specs=(vmem, vmem, vmem, vmem),
        scratch_shapes=[pltpu.VMEM(shape, kind) for shape, kind in scratch]
        + [dma(shape) for shape in sems],
        compiler_params=pltpu.CompilerParams(
            collective_id=0, has_side_effects=True, vmem_limit_bytes=56 << 20
        ),
        name="mixer",
    )(tok, ups, flog, fact, cval, cgate)


def complex_stack(factor):
    real_part = factor[0]
    imag_part = factor[1]
    return jnp.stack([jnp.stack([real_part, -imag_part]), jnp.stack([imag_part, real_part])])


def shards(
    tokens, upstream, conv_value, conv_gate, mix_one, mix_two, mix_three, mix_four, filter_log
):
    one = mix_one[:, 0].transpose(1, 0, 2).reshape(32, 1, 8, 128)
    signed = jnp.stack([mix_four[0, 0], -mix_four[1, 0]])
    four = signed.transpose(2, 0, 1).reshape(32, 1, 8, 128)
    wide = jnp.concatenate([one, four], axis=1).reshape(512, 128)
    two = complex_stack(mix_two).transpose(4, 2, 1, 0, 3).reshape(32, 1, 8, 64)
    three = complex_stack(mix_three).transpose(3, 2, 0, 1, 4).reshape(32, 1, 8, 64)
    narrow = jnp.concatenate([two, three], axis=1).reshape(512, 64)
    factors = jnp.concatenate([wide, jnp.pad(narrow, ((0, 0), (0, 64)))], axis=0)
    grad_x, grad_filter, grads, taps = mixer(
        tokens[0],
        upstream[0],
        filter_log.reshape(128, C),
        factors,
        conv_value,
        conv_gate,
    )
    taps = taps.transpose(1, 0, 2).reshape(8, C)
    outer = grads[:512].reshape(32, 2, 4, 2, 128)
    inner = grads[512:].reshape(32, 4, 2, 2, 32)
    grad_one = outer[:, 0].transpose(2, 0, 1, 3).reshape(2, 1, 128, 128)
    grad_four = outer[:, 1].transpose(2, 3, 0, 1).reshape(2, 1, 128, 128)
    grad_four = jnp.stack([grad_four[0], -grad_four[1]])
    grad_two = inner[:, :, 0].transpose(2, 1, 3, 0)
    grad_three = inner[:, :, 1].transpose(2, 1, 0, 3)
    return (
        grad_x[None],
        taps[0:3],
        taps[3:6],
        grad_one,
        grad_two,
        grad_three,
        grad_four,
        grad_filter.reshape(4, 32, C),
    )


def solution(mesh):
    inner = Mesh(mesh.devices.reshape(8, 2, 2, 16), ALL)
    rows = ("zl", "co")
    cols = ("zh", "xy")
    block = P(None, cols, None, None)
    return jax.shard_map(
        shards,
        mesh=inner,
        in_specs=(
            P(rows, cols, None),
            P(rows, cols, None),
            P(),
            P(),
            block,
            block,
            block,
            block,
            P(cols, None, None),
        ),
        out_specs=(
            P(rows, cols, None),
            P(),
            P(),
            block,
            block,
            block,
            block,
            P(cols, None, None),
        ),
        check_vma=False,
    )
```

```python
import jax
import jax.numpy as jnp
from jax import lax
from jax.experimental import pallas as pl
from jax.experimental.pallas import tpu as pltpu
from jax.sharding import Mesh, PartitionSpec as P

C = 1536
ALL = ("zl", "co", "zh", "xy")
MESH = pl.DeviceIdType.MESH
F32 = jnp.float32
BF16 = jnp.bfloat16
CHUNKS = 2
W = C // CHUNKS
TILE = 256
TILES = W // TILE


def iota(shape, dim):
    return lax.broadcasted_iota(jnp.int32, shape, dim)


def dot(a, b):
    return lax.dot_general(a, b, (((1,), (0,)), ((), ())), preferred_element_type=F32)


def dot_nt(a, b):
    return lax.dot_general(a, b, (((1,), (1,)), ((), ())), preferred_element_type=F32)


def await_bytes(ref, sem):
    pltpu.make_async_copy(ref, ref, sem).wait()


def kernel(
    tok,
    ups,
    flog,
    fact,
    cval,
    cgate,
    gx_out,
    gf_out,
    gg_out,
    cv_out,
    ts,
    us,
    fl,
    fa,
    halo,
    w14,
    w14t,
    bmat,
    bmatt,
    filt,
    ymat,
    xs,
    xr,
    vmat,
    zs,
    zr,
    ft,
    gbs,
    gws,
    dbm,
    dwm,
    vgs,
    ggs,
    es,
    er,
    gxs,
    rf,
    rb,
    rw,
    fin,
    gbf,
    gwf,
    cp,
    rc,
    cs,
    rz,
    ct,
    s_in,
    r_edge,
    r_t,
    r_u,
    s_fa,
    r_fa,
    s_halo,
    r_halo,
    s_x,
    r_x,
    s_z,
    r_z,
    s_e,
    r_e,
    s_out,
    r_out,
    s_rf,
    r_rf,
    s_rb,
    r_rb,
    s_rw,
    r_rw,
    s_gf,
    r_gf,
    s_gb,
    r_gb,
    s_gw,
    r_gw,
    s_sib,
    s_c1,
    r_c1,
    s_c2,
    r_c2,
    s_c3,
    r_c3,
):
    zl, co, zh, xy = (lax.axis_index(name) for name in ALL)
    me = co * 16 + xy
    z = zh * 8 + zl
    native = co == zh
    partner = (zl, 1 - co, 1 - zh, xy)
    sibling = (zl, 1 - co, zh, xy)

    def plane(j):
        return (zl, j // 16, zh, lax.rem(j, 16))

    def ring(k):
        return (lax.rem(k, 8), co, k // 8, xy)

    def remote(src, dst, ss, rs, dev):
        return pltpu.make_async_remote_copy(
            src_ref=src, dst_ref=dst, send_sem=ss, recv_sem=rs, device_id=dev, device_id_type=MESH
        )

    up = lax.rem(z + 1, 16)
    down = lax.rem(z + 15, 16)

    barrier = pltpu.get_barrier_semaphore()

    def greet_plane(i, carry):
        pl.semaphore_signal(
            barrier, inc=1, device_id=plane(lax.rem(me + i, 32)), device_id_type=MESH
        )
        return carry

    def greet_ring(i, carry):
        pl.semaphore_signal(
            barrier, inc=1, device_id=ring(lax.rem(z + i, 16)), device_id_type=MESH
        )
        return carry

    pl.semaphore_signal(barrier, inc=1, device_id=partner, device_id_type=MESH)
    lax.fori_loop(1, 16, greet_ring, 0)
    lax.fori_loop(1, 32, greet_plane, 0)
    pl.semaphore_wait(barrier, 47)

    def role_copies():
        out = []
        for lo, hi in ((0, 16), (112, 128)):
            part = pl.ds(lo, hi - lo)
            out.append((tok.at[part], ts.at[part], r_edge))
        for n in range(CHUNKS):
            cols = pl.ds(n * W, W)
            mid = pl.ds(16, 96)
            out.append((tok.at[mid, cols], ts.at[mid, cols], r_t.at[n]))
            out.append((ups.at[:, cols], us.at[:, cols], r_u.at[n]))
        return out

    @pl.when(native)
    def _():
        pltpu.make_async_copy(fact, fa, r_fa.at[0]).start()
        pltpu.make_async_copy(flog, fl, r_fa.at[1]).start()
        for src, dst, sem in role_copies():
            pltpu.make_async_copy(src, dst, sem).start()

        @pl.when(zl == 0)
        def _():
            remote(fact, fa, s_fa.at[0], r_fa.at[0], ring(down)).start()
            remote(flog, fl, s_fa.at[1], r_fa.at[1], ring(down)).start()

        @pl.when(zl == 7)
        def _():
            remote(fact, fa, s_fa.at[0], r_fa.at[0], ring(up)).start()
            remote(flog, fl, s_fa.at[1], r_fa.at[1], ring(up)).start()

    def swap_in(lo, hi):
        for i, (src, dst, sem) in enumerate(role_copies()):
            if lo <= i < hi:
                remote(src, dst, s_in.at[i], sem, partner).start()

    def swap_left(lo, hi):
        for i, (src, dst, sem) in enumerate(role_copies()):
            if lo <= i < hi:
                await_bytes(dst, s_in.at[i])

    @pl.when(jnp.logical_not(native))
    def _():
        swap_in(0, 4)

    def forward(src, slot):
        @pl.when(jnp.logical_not(native) & (zl < 3))
        def _():
            remote(src, src, s_fa.at[slot], r_fa.at[slot], ring(up)).start()

        @pl.when(jnp.logical_not(native) & (zl > 4))
        def _():
            remote(src, src, s_fa.at[slot], r_fa.at[slot], ring(down)).start()

    await_bytes(ts.at[pl.ds(0, 32)], r_edge)

    @pl.when(me > 0)
    def _():
        remote(ts.at[pl.ds(0, 16)], halo.at[1], s_halo.at[0], r_halo.at[1], plane(me - 1)).start()

    @pl.when(me < 31)
    def _():
        remote(
            ts.at[pl.ds(112, 16)], halo.at[0], s_halo.at[1], r_halo.at[0], plane(me + 1)
        ).start()

    await_bytes(fa, r_fa.at[0])
    forward(fa, 0)
    wc = fa[pl.ds(0, 512), :]
    first_row = lax.rem(iota((512, 128), 0) // 8, 2) == 0
    zero = jnp.zeros_like(wc)
    w14[:, pl.ds(0, 128)] = jnp.where(first_row, wc, zero)
    w14[:, pl.ds(128, 128)] = jnp.where(first_row, zero, wc)
    eye = (iota((128, 128), 0) == iota((128, 128), 1)).astype(BF16)
    wct = dot_nt(eye, wc)
    first_col = lax.rem(iota((128, 512), 1) // 8, 2) == 0
    w14t[pl.ds(0, 128), :] = jnp.where(first_col, wct, 0.0).astype(BF16)
    w14t[pl.ds(128, 128), :] = jnp.where(first_col, 0.0, wct).astype(BF16)

    def block_mask(rows, cols):
        return (lax.rem(rows // 8, 2) == cols // 256) & (
            lax.rem(rows // 2, 4) == lax.rem(cols // 32, 4)
        )

    dc = fa[pl.ds(512, 512), :]
    for n in range(4):
        part = pl.ds(n * 128, 128)
        s = iota((128, 128), 1) + n * 128
        l = iota((128, 128), 0)
        spread = (l == lax.rem(s // 128, 2) * 32 + lax.rem(s, 32)).astype(BF16)
        wide = dot(dc, spread)
        keep = block_mask(iota((512, 128), 0), iota((512, 128), 1) + n * 128)
        bmat[:, part] = jnp.where(keep, wide, 0.0).astype(BF16)
        s = iota((128, 128), 0) + n * 128
        l = iota((128, 128), 1)
        spread = (l == lax.rem(s // 128, 2) * 32 + lax.rem(s, 32)).astype(BF16)
        tall = dot_nt(spread, dc)
        keep = block_mask(iota((128, 512), 1), iota((128, 512), 0) + n * 128)
        bmatt[part, :] = jnp.where(keep, tall, 0.0).astype(BF16)

    dbm[...] = jnp.zeros_like(dbm)
    dwm[...] = jnp.zeros_like(dwm)

    @pl.when(me == 0)
    def _():
        halo[0] = jnp.zeros((16, C), BF16)

    @pl.when(me == 31)
    def _():
        halo[1] = jnp.zeros((16, C), BF16)

    @pl.when(me > 0)
    def _():
        await_bytes(halo.at[0], r_halo.at[0])

    @pl.when(me < 31)
    def _():
        await_bytes(halo.at[1], r_halo.at[1])

    rows = iota((128, TILE), 0)

    def shifted(x, before, after):
        prev = jnp.where(rows == 0, before, pltpu.roll(x, 1, axis=0))
        nxt = jnp.where(rows == 127, after, pltpu.roll(x, 127, axis=0))
        return prev, nxt

    def token_windows(cols):
        x = ts[:, cols].astype(F32)
        before = halo[0, :, cols].astype(F32)[15:16]
        after = halo[1, :, cols].astype(F32)[0:1]
        prev, nxt = shifted(x, before, after)
        return prev, x, nxt

    def tile_cols(n, i):
        return pl.ds(pl.multiple_of(n * W + i * TILE, TILE), TILE)

    def all_to_all(src, dst, ss, rs, n):
        cols = pl.ds(n * W, W)

        def send(i, carry):
            j = lax.rem(me + i, 32)
            remote(src.at[j, :, cols], dst.at[me, :, cols], ss.at[n], rs.at[n], plane(j)).start()
            return carry

        lax.fori_loop(1, 32, send, 0)
        pltpu.make_async_copy(src.at[me, :, cols], dst.at[me, :, cols], rs.at[n]).start()

    def phase_one(n):
        part = pl.ds(n * W, W)

        if n + 1 < CHUNKS:

            @pl.when(jnp.logical_not(native))
            def _():
                swap_left(2 * n + 2, 2 * n + 4)
                swap_in(2 * n + 4, 2 * n + 6)

        await_bytes(ts.at[pl.ds(16, 96), part], r_t.at[n])
        await_bytes(us.at[:, part], r_u.at[n])

        def tile(i, carry):
            cols = tile_cols(n, i)
            prev, x, nxt = token_windows(cols)
            cv = cval[:, cols]
            cg = cgate[:, cols]
            values = cv[0:1] * prev + cv[1:2] * x + cv[2:3] * nxt
            gating = (cg[0:1] * prev + cg[1:2] * x + cg[2:3] * nxt).astype(BF16).astype(F32)
            mix = us[:, cols].astype(F32) * gating
            ymat[pl.ds(0, 128), cols] = values.astype(BF16)
            ymat[pl.ds(128, 128), cols] = mix.astype(BF16)
            y = ymat[:, cols]
            xs[:, :, cols] = dot(w14[...], y).astype(BF16).reshape(32, 16, TILE)
            return carry

        lax.fori_loop(0, TILES, tile, 0)
        all_to_all(xs, xr, s_x, r_x, n)

    def reduce_send(src, size, dst, ss, rs):
        def send(k, carry):
            piece = src(pl.ds(pl.multiple_of(k * size, size), size))
            mine = native & (k == zl)

            @pl.when(mine)
            def _():
                pltpu.make_async_copy(piece, dst, rs).start()

            @pl.when(jnp.logical_not(mine))
            def _():
                remote(piece, dst, ss, rs, (k, co, co, xy)).start()

            return carry

        lax.fori_loop(0, 8, send, 0)

    def gather_send(src, dst, ss, rs):
        pltpu.make_async_copy(src, dst, rs).start()

        def send(i, carry):
            k = lax.rem(zl + i, 8)
            remote(src, dst, ss, rs, (k, co, co, xy)).start()
            return carry

        lax.fori_loop(1, 8, send, 0)

    def phase_two(n):
        part = pl.ds(n * W, W)
        await_bytes(xr.at[:, :, part], r_x.at[n])

        def tile(i, carry):
            cols = tile_cols(n, i)
            x = xr[:, :, cols].reshape(512, TILE)
            both = dot(bmatt[...], x)
            f = jnp.exp(fl[:, cols].astype(F32))
            filt[:, cols] = f
            sr = both[0:128]
            si = both[128:256]
            gr = both[256:384]
            gi = both[384:512]
            ft[:, cols] = (gr * sr + gi * si).astype(BF16)
            vmat[pl.ds(0, 128), cols] = (f * gr).astype(BF16)
            vmat[pl.ds(128, 128), cols] = (f * gi).astype(BF16)
            vmat[pl.ds(256, 128), cols] = (f * sr).astype(BF16)
            vmat[pl.ds(384, 128), cols] = (f * si).astype(BF16)
            v = vmat[:, cols]
            zs[:, :, cols] = dot(bmat[...], v).astype(BF16).reshape(32, 16, TILE)
            return carry

        lax.fori_loop(0, TILES, tile, 0)
        all_to_all(zs, zr, s_z, r_z, n)
        reduce_send(lambda piece: ft.at[piece, part], 16, rf.at[z, :, part], s_rf.at[n], r_rf.at[n])

        def tile_grad(i, carry):
            cols = tile_cols(n, i)
            dbm[...] += dot_nt(xr[:, :, cols].reshape(512, TILE), vmat[:, cols])
            return carry

        lax.fori_loop(0, TILES, tile_grad, 0)

    def phase_three(n):
        part = pl.ds(n * W, W)
        await_bytes(zr.at[:, :, part], r_z.at[n])

        def tile(i, carry):
            cols = tile_cols(n, i)
            zt = zr[:, :, cols].reshape(512, TILE)
            both = dot(w14t[...], zt)
            vg = both[0:128]
            gg = us[:, cols].astype(F32) * both[128:256]
            vgs[:, cols] = vg
            ggs[:, cols] = gg
            cv = cval[:, cols]
            cg = cgate[:, cols]
            es[0, :, cols] = jnp.broadcast_to(cv[0:1] * vg[0:1] + cg[0:1] * gg[0:1], (8, TILE))
            es[1, :, cols] = jnp.broadcast_to(
                cv[2:3] * vg[127:128] + cg[2:3] * gg[127:128], (8, TILE)
            )
            return carry

        lax.fori_loop(0, TILES, tile, 0)

        @pl.when(me > 0)
        def _():
            remote(
                es.at[0, :, part], er.at[1, :, part], s_e.at[n, 0], r_e.at[n, 1], plane(me - 1)
            ).start()

        @pl.when(me < 31)
        def _():
            remote(
                es.at[1, :, part], er.at[0, :, part], s_e.at[n, 1], r_e.at[n, 0], plane(me + 1)
            ).start()

        def tile_grad(i, carry):
            cols = tile_cols(n, i)
            prev, x, nxt = token_windows(cols)
            row = lax.broadcasted_iota(jnp.int32, (8, TILE), 0)
            total = jnp.zeros((8, TILE), F32)
            for at, grad in ((0, vgs[:, cols]), (3, ggs[:, cols])):
                for o, window in enumerate((prev, x, nxt)):
                    total += jnp.where(
                        row == at + o, jnp.sum(grad * window, axis=0, keepdims=True), 0.0
                    )
            for k in range(TILE // 128):
                cp[(n * W + i * TILE) // 128 + k] = total[:, k * 128 : (k + 1) * 128]
            dwm[...] += dot_nt(zr[:, :, cols].reshape(512, TILE), ymat[:, cols])
            return carry

        lax.fori_loop(0, TILES, tile_grad, 0)

    def phase_out(n):
        part = pl.ds(n * W, W)

        @pl.when(me == 0)
        def _():
            er[0, :, part] = jnp.zeros((8, W), F32)

        @pl.when(me == 31)
        def _():
            er[1, :, part] = jnp.zeros((8, W), F32)

        @pl.when(me > 0)
        def _():
            await_bytes(er.at[0, :, part], r_e.at[n, 0])

        @pl.when(me < 31)
        def _():
            await_bytes(er.at[1, :, part], r_e.at[n, 1])

        def tile(i, carry):
            cols = tile_cols(n, i)
            cv = cval[:, cols]
            cg = cgate[:, cols]
            vg = vgs[:, cols]
            gg = ggs[:, cols]
            ahead = cv[0:1] * vg + cg[0:1] * gg
            behind = cv[2:3] * vg + cg[2:3] * gg
            here = cv[1:2] * vg + cg[1:2] * gg
            first = er[0, :, cols][0:1]
            last = er[1, :, cols][0:1]
            down_rows = jnp.where(rows == 0, first, pltpu.roll(behind, 1, axis=0))
            up_rows = jnp.where(rows == 127, last, pltpu.roll(ahead, 127, axis=0))
            gxs[:, cols] = (up_rows + here + down_rows).astype(BF16)
            return carry

        lax.fori_loop(0, TILES, tile, 0)

        @pl.when(native)
        def _():
            pltpu.make_async_copy(gxs.at[:, part], gx_out.at[:, part], r_out.at[n]).start()

        @pl.when(jnp.logical_not(native))
        def _():
            remote(
                gxs.at[:, part], gx_out.at[:, part], s_out.at[n], r_out.at[n], partner
            ).start()

    def filter_finish(n):
        part = pl.ds(n * W, W)

        @pl.when(native)
        def _():
            await_bytes(rf.at[:, :, part], r_rf.at[n])

            def tile(i, carry):
                cols = tile_cols(n, i)
                total = rf[0, :, cols].astype(F32)
                for k in range(1, 16):
                    total += rf[k, :, cols].astype(F32)
                share = filt[pl.ds(pl.multiple_of(zl * 16, 16), 16), cols]
                fin[:, cols] = (share * total).astype(BF16)
                return carry

            lax.fori_loop(0, TILES, tile, 0)
            mine = pl.ds(pl.multiple_of(zl * 16, 16), 16)
            gather_send(fin.at[:, part], gf_out.at[mine, part], s_gf.at[n], r_gf.at[n])

    def inner_grads():
        keep_rows = iota((512, 128), 0)
        packed = [jnp.zeros((512, 128), F32), jnp.zeros((512, 128), F32)]
        for n in range(4):
            part = pl.ds(n * 128, 128)
            keep = block_mask(keep_rows, iota((512, 128), 1) + n * 128)
            q = jnp.where(keep, dbm[:, part], 0.0).astype(BF16)
            s = iota((128, 128), 0) + n * 128
            l = iota((128, 128), 1)
            same = (s // 256 == l // 64) & (lax.rem(s, 32) == lax.rem(l, 32))
            part_of = lax.rem(s // 128, 2)
            imag = lax.rem(l // 32, 2)
            for p in range(2):
                hit = same & (part_of == (imag if p == 0 else 1 - imag))
                minus = (imag == 1) & (l // 64 != p)
                sel = jnp.where(hit, jnp.where(minus, -1.0, 1.0), 0.0).astype(BF16)
                packed[p] = packed[p] + dot(q, sel)
        gb = jnp.zeros((128, 128), F32)
        a = iota((128, 512), 0)
        r = iota((128, 512), 1)
        for p in range(2):
            pick = (r // 16 == a // 4) & (lax.rem(r // 2, 4) == lax.rem(a, 4)) & (lax.rem(r, 2) == p)
            gb = gb + dot(pick.astype(BF16), packed[p].astype(BF16))
        gbs[...] = gb.astype(BF16)
        reduce_send(lambda piece: gbs.at[piece], 16, rb.at[z], s_rb, r_rb)

    def filter_in():
        await_bytes(fl, r_fa.at[1])
        forward(fl, 1)

    for n in range(CHUNKS):
        phase_one(n)
    filter_in()
    for n in range(CHUNKS):
        phase_two(n)
    inner_grads()
    for n in range(CHUNKS):
        phase_three(n)
        if n + 1 < CHUNKS:
            phase_out(n)

    def tap_send(k, carry):
        @pl.when(k == me)
        def _():
            pltpu.make_async_copy(cp.at[k], rc.at[me], r_c1).start()

        @pl.when(k != me)
        def _():
            remote(cp.at[k], rc.at[me], s_c1, r_c1, plane(k)).start()

        return carry

    lax.fori_loop(0, 12, tap_send, 0)

    phase_out(CHUNKS - 1)

    t_first = lax.rem(iota((512, 128), 0) // 8, 2) == 0
    gws[...] = jnp.where(t_first, dwm[:, pl.ds(0, 128)], dwm[:, pl.ds(128, 128)]).astype(BF16)
    reduce_send(lambda piece: gws.at[piece], 64, rw.at[z], s_rw, r_rw)

    owner = me < 12

    @pl.when(owner)
    def _():
        await_bytes(rc, r_c1)
        cs[...] = jnp.sum(rc[...], axis=0)
        pltpu.make_async_copy(cs, rz.at[z], r_c2).start()

        def send(i, carry):
            remote(cs, rz.at[z], s_c2, r_c2, ring(lax.rem(z + i, 16))).start()
            return carry

        lax.fori_loop(1, 16, send, 0)

    for n in range(CHUNKS):
        filter_finish(n)

    @pl.when(native)
    def _():
        await_bytes(rb, r_rb)
        total = rb[0].astype(F32)
        for k in range(1, 16):
            total += rb[k].astype(F32)
        gbf[...] = total.astype(BF16)
        row = pl.ds(pl.multiple_of(512 + zl * 16, 16), 16)
        gather_send(gbf, gg_out.at[row], s_gb, r_gb)

    @pl.when(native)
    def _():
        await_bytes(rw, r_rw)
        total = rw[0].astype(F32)
        for k in range(1, 16):
            total += rw[k].astype(F32)
        gwf[...] = total.astype(BF16)
        row = pl.ds(pl.multiple_of(zl * 64, 64), 64)
        gather_send(gwf, gg_out.at[row], s_gw, r_gw)

    @pl.when(owner)
    def _():
        await_bytes(rz, r_c2)
        ct[...] = jnp.sum(rz[...], axis=0)
        pltpu.make_async_copy(ct, cv_out.at[me], r_c3).start()

        def send(i, carry):
            remote(ct, cv_out.at[me], s_c3, r_c3, plane(lax.rem(me + i, 32))).start()
            return carry

        lax.fori_loop(1, 32, send, 0)

    low = pl.ds(0, 512)
    high = pl.ds(512, 128)

    @pl.when(native)
    def _():
        for n in range(CHUNKS):
            part = pl.ds(n * W, W)
            await_bytes(gf_out.at[:, part], r_gf.at[n])
            remote(
                gf_out.at[:, part], gf_out.at[:, part], s_sib.at[n], r_gf.at[n], sibling
            ).start()
        await_bytes(gg_out.at[high], r_gb)
        remote(gg_out.at[high], gg_out.at[high], s_sib.at[CHUNKS], r_gb, sibling).start()
        await_bytes(gg_out.at[low], r_gw)
        remote(gg_out.at[low], gg_out.at[low], s_sib.at[CHUNKS + 1], r_gw, sibling).start()

    @pl.when(jnp.logical_not(native))
    def _():
        for n in range(CHUNKS):
            await_bytes(gf_out.at[:, pl.ds(n * W, W)], r_gf.at[n])
        await_bytes(gg_out.at[high], r_gb)
        await_bytes(gg_out.at[low], r_gw)

    await_bytes(cv_out, r_c3)
    for n in range(CHUNKS):
        await_bytes(gx_out.at[:, pl.ds(n * W, W)], r_out.at[n])

    @pl.when(jnp.logical_not(native))
    def _():
        swap_left(0, 2)
        swap_left(2 * CHUNKS, 2 * CHUNKS + 2)
        for n in range(CHUNKS):
            await_bytes(gxs.at[:, pl.ds(n * W, W)], s_out.at[n])

        @pl.when((zl < 3) | (zl > 4))
        def _():
            await_bytes(fa, s_fa.at[0])
            await_bytes(fl, s_fa.at[1])

    @pl.when(me > 0)
    def _():
        await_bytes(halo.at[1], s_halo.at[0])
        for n in range(CHUNKS):
            await_bytes(es.at[0, :, pl.ds(n * W, W)], s_e.at[n, 0])

    @pl.when(me < 31)
    def _():
        await_bytes(halo.at[0], s_halo.at[1])
        for n in range(CHUNKS):
            await_bytes(es.at[1, :, pl.ds(n * W, W)], s_e.at[n, 1])

    for n in range(CHUNKS):
        part = pl.ds(n * W, W)
        await_bytes(xs.at[pl.ds(0, 31), :, part], s_x.at[n])
        await_bytes(zs.at[pl.ds(0, 31), :, part], s_z.at[n])

    @pl.when(native)
    def _():
        @pl.when((zl == 0) | (zl == 7))
        def _():
            await_bytes(fa, s_fa.at[0])
            await_bytes(fl, s_fa.at[1])

        for n in range(CHUNKS):
            part = pl.ds(n * W, W)
            await_bytes(ft.at[pl.ds(0, 112), part], s_rf.at[n])
            await_bytes(gf_out.at[pl.ds(0, 112), part], s_gf.at[n])
            await_bytes(gf_out.at[:, part], s_sib.at[n])
        await_bytes(gbs.at[pl.ds(0, 112)], s_rb)
        await_bytes(gws.at[pl.ds(0, 448)], s_rw)
        await_bytes(gbs.at[pl.ds(0, 112)], s_gb)
        await_bytes(gws.at[pl.ds(0, 448)], s_gw)
        await_bytes(gg_out.at[high], s_sib.at[CHUNKS])
        await_bytes(gg_out.at[low], s_sib.at[CHUNKS + 1])

    @pl.when(jnp.logical_not(native))
    def _():
        for n in range(CHUNKS):
            await_bytes(ft.at[:, pl.ds(n * W, W)], s_rf.at[n])
        await_bytes(gbs, s_rb)
        await_bytes(gws, s_rw)

    @pl.when(owner)
    def _():
        await_bytes(cp.at[pl.ds(0, 11)], s_c1)
        await_bytes(rz.at[pl.ds(0, 15)], s_c2)
        await_bytes(rc.at[pl.ds(0, 31)], s_c3)

    @pl.when(jnp.logical_not(owner))
    def _():
        await_bytes(cp, s_c1)


def mixer(tok, ups, flog, fact, cval, cgate):
    vmem = pl.BlockSpec(memory_space=pltpu.VMEM)
    hbm = pl.BlockSpec(memory_space=pl.ANY)
    dma = pltpu.SemaphoreType.DMA
    scratch = [
        ((128, C), BF16),
        ((128, C), BF16),
        ((128, C), BF16),
        ((1024, 128), BF16),
        ((2, 16, C), BF16),
        ((512, 256), BF16),
        ((256, 512), BF16),
        ((512, 512), BF16),
        ((512, 512), BF16),
        ((128, C), F32),
        ((256, C), BF16),
        ((32, 16, C), BF16),
        ((32, 16, C), BF16),
        ((512, C), BF16),
        ((32, 16, C), BF16),
        ((32, 16, C), BF16),
        ((128, C), BF16),
        ((128, 128), BF16),
        ((512, 128), BF16),
        ((512, 512), F32),
        ((512, 256), F32),
        ((128, C), F32),
        ((128, C), F32),
        ((2, 8, C), F32),
        ((2, 8, C), F32),
        ((128, C), BF16),
        ((16, 16, C), BF16),
        ((16, 16, 128), BF16),
        ((16, 64, 128), BF16),
        ((16, C), BF16),
        ((16, 128), BF16),
        ((64, 128), BF16),
        ((12, 8, 128), F32),
        ((32, 8, 128), F32),
        ((8, 128), F32),
        ((16, 8, 128), F32),
        ((8, 128), F32),
    ]
    n = CHUNKS
    sems = [
        (2 + 2 * n,),
        (),
        (n,),
        (n,),
        (2,),
        (2,),
        (2,),
        (2,),
        (n,),
        (n,),
        (n,),
        (n,),
        (n, 2),
        (n, 2),
        (n,),
        (n,),
        (n,),
        (n,),
        (),
        (),
        (),
        (),
        (n,),
        (n,),
        (),
        (),
        (),
        (),
        (n + 2,),
        (),
        (),
        (),
        (),
        (),
        (),
    ]
    return pl.pallas_call(
        kernel,
        out_shape=(
            jax.ShapeDtypeStruct((128, C), BF16),
            jax.ShapeDtypeStruct((128, C), BF16),
            jax.ShapeDtypeStruct((640, 128), BF16),
            jax.ShapeDtypeStruct((12, 8, 128), F32),
        ),
        in_specs=[hbm, hbm, hbm, hbm, vmem, vmem],
        out_specs=(vmem, vmem, vmem, vmem),
        scratch_shapes=[pltpu.VMEM(shape, kind) for shape, kind in scratch]
        + [dma(shape) for shape in sems],
        compiler_params=pltpu.CompilerParams(
            collective_id=0, has_side_effects=True, vmem_limit_bytes=56 << 20
        ),
        name="mixer",
    )(tok, ups, flog, fact, cval, cgate)


def complex_stack(factor):
    real_part = factor[0]
    imag_part = factor[1]
    return jnp.stack([jnp.stack([real_part, -imag_part]), jnp.stack([imag_part, real_part])])


def shards(
    tokens, upstream, conv_value, conv_gate, mix_one, mix_two, mix_three, mix_four, filter_log
):
    one = mix_one[:, 0].transpose(1, 0, 2).reshape(32, 1, 8, 128)
    signed = jnp.stack([mix_four[0, 0], -mix_four[1, 0]])
    four = signed.transpose(2, 0, 1).reshape(32, 1, 8, 128)
    wide = jnp.concatenate([one, four], axis=1).reshape(512, 128)
    two = complex_stack(mix_two).transpose(4, 2, 1, 0, 3).reshape(32, 1, 8, 64)
    three = complex_stack(mix_three).transpose(3, 2, 0, 1, 4).reshape(32, 1, 8, 64)
    narrow = jnp.concatenate([two, three], axis=1).reshape(512, 64)
    factors = jnp.concatenate([wide, jnp.pad(narrow, ((0, 0), (0, 64)))], axis=0)
    grad_x, grad_filter, grads, taps = mixer(
        tokens[0],
        upstream[0],
        filter_log.reshape(128, C),
        factors,
        conv_value,
        conv_gate,
    )
    taps = taps.transpose(1, 0, 2).reshape(8, C)
    outer = grads[:512].reshape(32, 2, 4, 2, 128)
    inner = grads[512:].reshape(32, 4, 2, 2, 32)
    grad_one = outer[:, 0].transpose(2, 0, 1, 3).reshape(2, 1, 128, 128)
    grad_four = outer[:, 1].transpose(2, 3, 0, 1).reshape(2, 1, 128, 128)
    grad_four = jnp.stack([grad_four[0], -grad_four[1]])
    grad_two = inner[:, :, 0].transpose(2, 1, 3, 0)
    grad_three = inner[:, :, 1].transpose(2, 1, 0, 3)
    return (
        grad_x[None],
        taps[0:3],
        taps[3:6],
        grad_one,
        grad_two,
        grad_three,
        grad_four,
        grad_filter.reshape(4, 32, C),
    )


def solution(mesh):
    inner = Mesh(mesh.devices.reshape(8, 2, 2, 16), ALL)
    rows = ("zl", "co")
    cols = ("zh", "xy")
    block = P(None, cols, None, None)
    return jax.shard_map(
        shards,
        mesh=inner,
        in_specs=(
            P(rows, cols, None),
            P(rows, cols, None),
            P(),
            P(),
            block,
            block,
            block,
            block,
            P(cols, None, None),
        ),
        out_specs=(
            P(rows, cols, None),
            P(),
            P(),
            block,
            block,
            block,
            block,
            P(cols, None, None),
        ),
        check_vma=False,
    )
```

```python
import jax
import jax.numpy as jnp
from jax import lax
from jax.experimental import pallas as pl
from jax.experimental.pallas import tpu as pltpu
from jax.sharding import Mesh, PartitionSpec as P

C = 1536
ALL = ("zl", "co", "zh", "xy")
MESH = pl.DeviceIdType.MESH
F32 = jnp.float32
BF16 = jnp.bfloat16
CHUNKS = 2
W = C // CHUNKS
TILE = 256
TILES = W // TILE


def iota(shape, dim):
    return lax.broadcasted_iota(jnp.int32, shape, dim)


def dot(a, b):
    return lax.dot_general(a, b, (((1,), (0,)), ((), ())), preferred_element_type=F32)


def dot_nt(a, b):
    return lax.dot_general(a, b, (((1,), (1,)), ((), ())), preferred_element_type=F32)


def await_bytes(ref, sem):
    pltpu.make_async_copy(ref, ref, sem).wait()


def kernel(
    tok,
    ups,
    flog,
    fact,
    cval,
    cgate,
    gx_out,
    gf_out,
    one_out,
    four_out,
    two_out,
    three_out,
    tapv_out,
    tapg_out,
    gg,
    cvs,
    ts,
    us,
    fl,
    fa,
    halo,
    w14,
    w14t,
    bmat,
    bmatt,
    filt,
    ymat,
    xs,
    xr,
    vmat,
    zs,
    zr,
    ft,
    gbs,
    gws,
    dbm,
    dwm,
    vgs,
    ggs,
    es,
    er,
    gxs,
    rf,
    rb,
    rw,
    fin,
    gbf,
    gwf,
    cp,
    rc,
    cs,
    rz,
    ct,
    s_in,
    r_edge,
    r_t,
    r_u,
    s_fa,
    r_fa,
    s_halo,
    r_halo,
    s_x,
    r_x,
    s_z,
    r_z,
    s_e,
    r_e,
    s_out,
    r_out,
    s_rf,
    r_rf,
    s_rb,
    r_rb,
    s_rw,
    r_rw,
    s_gf,
    r_gf,
    s_gb,
    r_gb,
    s_gw,
    r_gw,
    s_sib,
    s_c1,
    r_c1,
    s_c2,
    r_c2,
    s_c3,
    r_c3,
):
    zl, co, zh, xy = (lax.axis_index(name) for name in ALL)
    me = co * 16 + xy
    z = zh * 8 + zl
    native = co == zh
    partner = (zl, 1 - co, 1 - zh, xy)
    sibling = (zl, 1 - co, zh, xy)

    def plane(j):
        return (zl, j // 16, zh, lax.rem(j, 16))

    def ring(k):
        return (lax.rem(k, 8), co, k // 8, xy)

    def remote(src, dst, ss, rs, dev):
        return pltpu.make_async_remote_copy(
            src_ref=src, dst_ref=dst, send_sem=ss, recv_sem=rs, device_id=dev, device_id_type=MESH
        )

    up = lax.rem(z + 1, 16)
    down = lax.rem(z + 15, 16)

    barrier = pltpu.get_barrier_semaphore()

    def greet_plane(i, carry):
        pl.semaphore_signal(
            barrier, inc=1, device_id=plane(lax.rem(me + i, 32)), device_id_type=MESH
        )
        return carry

    def greet_ring(i, carry):
        pl.semaphore_signal(
            barrier, inc=1, device_id=ring(lax.rem(z + i, 16)), device_id_type=MESH
        )
        return carry

    pl.semaphore_signal(barrier, inc=1, device_id=partner, device_id_type=MESH)
    lax.fori_loop(1, 16, greet_ring, 0)
    lax.fori_loop(1, 32, greet_plane, 0)
    pl.semaphore_wait(barrier, 47)

    def role_copies():
        out = []
        for lo, hi in ((0, 16), (112, 128)):
            part = pl.ds(lo, hi - lo)
            out.append((tok.at[part], ts.at[part], r_edge))
        for n in range(CHUNKS):
            cols = pl.ds(n * W, W)
            mid = pl.ds(16, 96)
            out.append((tok.at[mid, cols], ts.at[mid, cols], r_t.at[n]))
            out.append((ups.at[:, cols], us.at[:, cols], r_u.at[n]))
        return out

    @pl.when(native)
    def _():
        pltpu.make_async_copy(fact, fa, r_fa.at[0]).start()
        pltpu.make_async_copy(flog, fl, r_fa.at[1]).start()
        for src, dst, sem in role_copies():
            pltpu.make_async_copy(src, dst, sem).start()

        @pl.when(zl == 0)
        def _():
            remote(fact, fa, s_fa.at[0], r_fa.at[0], ring(down)).start()
            remote(flog, fl, s_fa.at[1], r_fa.at[1], ring(down)).start()

        @pl.when(zl == 7)
        def _():
            remote(fact, fa, s_fa.at[0], r_fa.at[0], ring(up)).start()
            remote(flog, fl, s_fa.at[1], r_fa.at[1], ring(up)).start()

    def swap_in(lo, hi):
        for i, (src, dst, sem) in enumerate(role_copies()):
            if lo <= i < hi:
                remote(src, dst, s_in.at[i], sem, partner).start()

    def swap_left(lo, hi):
        for i, (src, dst, sem) in enumerate(role_copies()):
            if lo <= i < hi:
                await_bytes(dst, s_in.at[i])

    @pl.when(jnp.logical_not(native))
    def _():
        swap_in(0, 4)

    def forward(src, slot):
        @pl.when(jnp.logical_not(native) & (zl < 3))
        def _():
            remote(src, src, s_fa.at[slot], r_fa.at[slot], ring(up)).start()

        @pl.when(jnp.logical_not(native) & (zl > 4))
        def _():
            remote(src, src, s_fa.at[slot], r_fa.at[slot], ring(down)).start()

    await_bytes(ts.at[pl.ds(0, 32)], r_edge)

    @pl.when(me > 0)
    def _():
        remote(ts.at[pl.ds(0, 16)], halo.at[1], s_halo.at[0], r_halo.at[1], plane(me - 1)).start()

    @pl.when(me < 31)
    def _():
        remote(
            ts.at[pl.ds(112, 16)], halo.at[0], s_halo.at[1], r_halo.at[0], plane(me + 1)
        ).start()

    await_bytes(fa, r_fa.at[0])
    forward(fa, 0)
    wc = fa[pl.ds(0, 512), :]
    first_row = lax.rem(iota((512, 128), 0) // 8, 2) == 0
    zero = jnp.zeros_like(wc)
    w14[:, pl.ds(0, 128)] = jnp.where(first_row, wc, zero)
    w14[:, pl.ds(128, 128)] = jnp.where(first_row, zero, wc)
    eye = (iota((128, 128), 0) == iota((128, 128), 1)).astype(BF16)
    wct = dot_nt(eye, wc)
    first_col = lax.rem(iota((128, 512), 1) // 8, 2) == 0
    w14t[pl.ds(0, 128), :] = jnp.where(first_col, wct, 0.0).astype(BF16)
    w14t[pl.ds(128, 128), :] = jnp.where(first_col, 0.0, wct).astype(BF16)

    def block_mask(rows, cols):
        return (lax.rem(rows // 8, 2) == cols // 256) & (
            lax.rem(rows // 2, 4) == lax.rem(cols // 32, 4)
        )

    dc = fa[pl.ds(512, 512), :]
    for n in range(4):
        part = pl.ds(n * 128, 128)
        s = iota((128, 128), 1) + n * 128
        l = iota((128, 128), 0)
        spread = (l == lax.rem(s // 128, 2) * 32 + lax.rem(s, 32)).astype(BF16)
        wide = dot(dc, spread)
        keep = block_mask(iota((512, 128), 0), iota((512, 128), 1) + n * 128)
        bmat[:, part] = jnp.where(keep, wide, 0.0).astype(BF16)
        s = iota((128, 128), 0) + n * 128
        l = iota((128, 128), 1)
        spread = (l == lax.rem(s // 128, 2) * 32 + lax.rem(s, 32)).astype(BF16)
        tall = dot_nt(spread, dc)
        keep = block_mask(iota((128, 512), 1), iota((128, 512), 0) + n * 128)
        bmatt[part, :] = jnp.where(keep, tall, 0.0).astype(BF16)

    dbm[...] = jnp.zeros_like(dbm)
    dwm[...] = jnp.zeros_like(dwm)

    @pl.when(me == 0)
    def _():
        halo[0] = jnp.zeros((16, C), BF16)

    @pl.when(me == 31)
    def _():
        halo[1] = jnp.zeros((16, C), BF16)

    @pl.when(me > 0)
    def _():
        await_bytes(halo.at[0], r_halo.at[0])

    @pl.when(me < 31)
    def _():
        await_bytes(halo.at[1], r_halo.at[1])

    rows = iota((128, TILE), 0)

    def shifted(x, before, after):
        prev = jnp.where(rows == 0, before, pltpu.roll(x, 1, axis=0))
        nxt = jnp.where(rows == 127, after, pltpu.roll(x, 127, axis=0))
        return prev, nxt

    def token_windows(cols):
        x = ts[:, cols].astype(F32)
        before = halo[0, :, cols].astype(F32)[15:16]
        after = halo[1, :, cols].astype(F32)[0:1]
        prev, nxt = shifted(x, before, after)
        return prev, x, nxt

    def tile_cols(n, i):
        return pl.ds(pl.multiple_of(n * W + i * TILE, TILE), TILE)

    def all_to_all(src, dst, ss, rs, n):
        cols = pl.ds(n * W, W)

        def send(i, carry):
            j = lax.rem(me + i, 32)
            remote(src.at[j, :, cols], dst.at[me, :, cols], ss.at[n], rs.at[n], plane(j)).start()
            return carry

        lax.fori_loop(1, 32, send, 0)
        pltpu.make_async_copy(src.at[me, :, cols], dst.at[me, :, cols], rs.at[n]).start()

    def phase_one(n):
        part = pl.ds(n * W, W)

        if n + 1 < CHUNKS:

            @pl.when(jnp.logical_not(native))
            def _():
                swap_left(2 * n + 2, 2 * n + 4)
                swap_in(2 * n + 4, 2 * n + 6)

        await_bytes(ts.at[pl.ds(16, 96), part], r_t.at[n])
        await_bytes(us.at[:, part], r_u.at[n])

        def tile(i, carry):
            cols = tile_cols(n, i)
            prev, x, nxt = token_windows(cols)
            cv = cval[:, cols]
            cg = cgate[:, cols]
            values = cv[0:1] * prev + cv[1:2] * x + cv[2:3] * nxt
            gating = (cg[0:1] * prev + cg[1:2] * x + cg[2:3] * nxt).astype(BF16).astype(F32)
            mix = us[:, cols].astype(F32) * gating
            ymat[pl.ds(0, 128), cols] = values.astype(BF16)
            ymat[pl.ds(128, 128), cols] = mix.astype(BF16)
            y = ymat[:, cols]
            xs[:, :, cols] = dot(w14[...], y).astype(BF16).reshape(32, 16, TILE)
            return carry

        lax.fori_loop(0, TILES, tile, 0)
        all_to_all(xs, xr, s_x, r_x, n)

    def reduce_send(src, size, dst, ss, rs):
        def send(k, carry):
            piece = src(pl.ds(pl.multiple_of(k * size, size), size))
            mine = native & (k == zl)

            @pl.when(mine)
            def _():
                pltpu.make_async_copy(piece, dst, rs).start()

            @pl.when(jnp.logical_not(mine))
            def _():
                remote(piece, dst, ss, rs, (k, co, co, xy)).start()

            return carry

        lax.fori_loop(0, 8, send, 0)

    def gather_send(src, dst, ss, rs):
        pltpu.make_async_copy(src, dst, rs).start()

        def send(i, carry):
            k = lax.rem(zl + i, 8)
            remote(src, dst, ss, rs, (k, co, co, xy)).start()
            return carry

        lax.fori_loop(1, 8, send, 0)

    def phase_two(n):
        part = pl.ds(n * W, W)
        await_bytes(xr.at[:, :, part], r_x.at[n])

        def tile(i, carry):
            cols = tile_cols(n, i)
            x = xr[:, :, cols].reshape(512, TILE)
            both = dot(bmatt[...], x)
            f = jnp.exp(fl[:, cols].astype(F32))
            filt[:, cols] = f
            sr = both[0:128]
            si = both[128:256]
            gr = both[256:384]
            gi = both[384:512]
            ft[:, cols] = (gr * sr + gi * si).astype(BF16)
            vmat[pl.ds(0, 128), cols] = (f * gr).astype(BF16)
            vmat[pl.ds(128, 128), cols] = (f * gi).astype(BF16)
            vmat[pl.ds(256, 128), cols] = (f * sr).astype(BF16)
            vmat[pl.ds(384, 128), cols] = (f * si).astype(BF16)
            v = vmat[:, cols]
            zs[:, :, cols] = dot(bmat[...], v).astype(BF16).reshape(32, 16, TILE)
            return carry

        lax.fori_loop(0, TILES, tile, 0)
        all_to_all(zs, zr, s_z, r_z, n)
        reduce_send(lambda piece: ft.at[piece, part], 16, rf.at[z, :, part], s_rf.at[n], r_rf.at[n])

        def tile_grad(i, carry):
            cols = tile_cols(n, i)
            dbm[...] += dot_nt(xr[:, :, cols].reshape(512, TILE), vmat[:, cols])
            return carry

        lax.fori_loop(0, TILES, tile_grad, 0)

    def phase_three(n):
        part = pl.ds(n * W, W)
        await_bytes(zr.at[:, :, part], r_z.at[n])

        def tile(i, carry):
            cols = tile_cols(n, i)
            zt = zr[:, :, cols].reshape(512, TILE)
            both = dot(w14t[...], zt)
            vg = both[0:128]
            gg = us[:, cols].astype(F32) * both[128:256]
            vgs[:, cols] = vg
            ggs[:, cols] = gg
            cv = cval[:, cols]
            cg = cgate[:, cols]
            es[0, :, cols] = jnp.broadcast_to(cv[0:1] * vg[0:1] + cg[0:1] * gg[0:1], (8, TILE))
            es[1, :, cols] = jnp.broadcast_to(
                cv[2:3] * vg[127:128] + cg[2:3] * gg[127:128], (8, TILE)
            )
            return carry

        lax.fori_loop(0, TILES, tile, 0)

        @pl.when(me > 0)
        def _():
            remote(
                es.at[0, :, part], er.at[1, :, part], s_e.at[n, 0], r_e.at[n, 1], plane(me - 1)
            ).start()

        @pl.when(me < 31)
        def _():
            remote(
                es.at[1, :, part], er.at[0, :, part], s_e.at[n, 1], r_e.at[n, 0], plane(me + 1)
            ).start()

        def tile_grad(i, carry):
            cols = tile_cols(n, i)
            prev, x, nxt = token_windows(cols)
            row = lax.broadcasted_iota(jnp.int32, (8, TILE), 0)
            total = jnp.zeros((8, TILE), F32)
            for at, grad in ((0, vgs[:, cols]), (3, ggs[:, cols])):
                for o, window in enumerate((prev, x, nxt)):
                    total += jnp.where(
                        row == at + o, jnp.sum(grad * window, axis=0, keepdims=True), 0.0
                    )
            for k in range(TILE // 128):
                cp[(n * W + i * TILE) // 128 + k] = total[:, k * 128 : (k + 1) * 128]
            dwm[...] += dot_nt(zr[:, :, cols].reshape(512, TILE), ymat[:, cols])
            return carry

        lax.fori_loop(0, TILES, tile_grad, 0)

    def phase_out(n):
        part = pl.ds(n * W, W)

        @pl.when(me == 0)
        def _():
            er[0, :, part] = jnp.zeros((8, W), F32)

        @pl.when(me == 31)
        def _():
            er[1, :, part] = jnp.zeros((8, W), F32)

        @pl.when(me > 0)
        def _():
            await_bytes(er.at[0, :, part], r_e.at[n, 0])

        @pl.when(me < 31)
        def _():
            await_bytes(er.at[1, :, part], r_e.at[n, 1])

        def tile(i, carry):
            cols = tile_cols(n, i)
            cv = cval[:, cols]
            cg = cgate[:, cols]
            vg = vgs[:, cols]
            gg = ggs[:, cols]
            ahead = cv[0:1] * vg + cg[0:1] * gg
            behind = cv[2:3] * vg + cg[2:3] * gg
            here = cv[1:2] * vg + cg[1:2] * gg
            first = er[0, :, cols][0:1]
            last = er[1, :, cols][0:1]
            down_rows = jnp.where(rows == 0, first, pltpu.roll(behind, 1, axis=0))
            up_rows = jnp.where(rows == 127, last, pltpu.roll(ahead, 127, axis=0))
            gxs[:, cols] = (up_rows + here + down_rows).astype(BF16)
            return carry

        lax.fori_loop(0, TILES, tile, 0)

        @pl.when(native)
        def _():
            pltpu.make_async_copy(gxs.at[:, part], gx_out.at[:, part], r_out.at[n]).start()

        @pl.when(jnp.logical_not(native))
        def _():
            remote(
                gxs.at[:, part], gx_out.at[:, part], s_out.at[n], r_out.at[n], partner
            ).start()

    def filter_finish(n):
        part = pl.ds(n * W, W)

        @pl.when(native)
        def _():
            await_bytes(rf.at[:, :, part], r_rf.at[n])

            def tile(i, carry):
                cols = tile_cols(n, i)
                total = rf[0, :, cols].astype(F32)
                for k in range(1, 16):
                    total += rf[k, :, cols].astype(F32)
                share = filt[pl.ds(pl.multiple_of(zl * 16, 16), 16), cols]
                fin[:, cols] = (share * total).astype(BF16)
                return carry

            lax.fori_loop(0, TILES, tile, 0)
            mine = pl.ds(pl.multiple_of(zl * 16, 16), 16)
            gather_send(fin.at[:, part], gf_out.at[mine, part], s_gf.at[n], r_gf.at[n])

    def inner_grads():
        keep_rows = iota((512, 128), 0)
        packed = [jnp.zeros((512, 128), F32), jnp.zeros((512, 128), F32)]
        for n in range(4):
            part = pl.ds(n * 128, 128)
            keep = block_mask(keep_rows, iota((512, 128), 1) + n * 128)
            q = jnp.where(keep, dbm[:, part], 0.0).astype(BF16)
            s = iota((128, 128), 0) + n * 128
            l = iota((128, 128), 1)
            same = (s // 256 == l // 64) & (lax.rem(s, 32) == lax.rem(l, 32))
            part_of = lax.rem(s // 128, 2)
            imag = lax.rem(l // 32, 2)
            for p in range(2):
                hit = same & (part_of == (imag if p == 0 else 1 - imag))
                minus = (imag == 1) & (l // 64 != p)
                sel = jnp.where(hit, jnp.where(minus, -1.0, 1.0), 0.0).astype(BF16)
                packed[p] = packed[p] + dot(q, sel)
        gb = jnp.zeros((128, 128), F32)
        a = iota((128, 512), 0)
        r = iota((128, 512), 1)
        for p in range(2):
            pick = (r // 16 == a // 4) & (lax.rem(r // 2, 4) == lax.rem(a, 4)) & (lax.rem(r, 2) == p)
            gb = gb + dot(pick.astype(BF16), packed[p].astype(BF16))
        gbs[...] = gb.astype(BF16)
        reduce_send(lambda piece: gbs.at[piece], 16, rb.at[z], s_rb, r_rb)

    def filter_in():
        await_bytes(fl, r_fa.at[1])
        forward(fl, 1)

    for n in range(CHUNKS):
        phase_one(n)
    filter_in()
    for n in range(CHUNKS):
        phase_two(n)
    inner_grads()
    for n in range(CHUNKS):
        phase_three(n)
        phase_out(n)
    for n in range(CHUNKS):
        filter_finish(n)

    t_first = lax.rem(iota((512, 128), 0) // 8, 2) == 0
    gws[...] = jnp.where(t_first, dwm[:, pl.ds(0, 128)], dwm[:, pl.ds(128, 128)]).astype(BF16)
    reduce_send(lambda piece: gws.at[piece], 64, rw.at[z], s_rw, r_rw)

    def tap_send(k, carry):
        @pl.when(k == me)
        def _():
            pltpu.make_async_copy(cp.at[k], rc.at[me], r_c1).start()

        @pl.when(k != me)
        def _():
            remote(cp.at[k], rc.at[me], s_c1, r_c1, plane(k)).start()

        return carry

    lax.fori_loop(0, 12, tap_send, 0)

    @pl.when(native)
    def _():
        await_bytes(rb, r_rb)
        total = rb[0].astype(F32)
        for k in range(1, 16):
            total += rb[k].astype(F32)
        gbf[...] = total.astype(BF16)
        row = pl.ds(pl.multiple_of(512 + zl * 16, 16), 16)
        gather_send(gbf, gg.at[row], s_gb, r_gb)

    owner = me < 12

    @pl.when(owner)
    def _():
        await_bytes(rc, r_c1)
        cs[...] = jnp.sum(rc[...], axis=0)
        pltpu.make_async_copy(cs, rz.at[z], r_c2).start()

        def send(i, carry):
            remote(cs, rz.at[z], s_c2, r_c2, ring(lax.rem(z + i, 16))).start()
            return carry

        lax.fori_loop(1, 16, send, 0)

    @pl.when(native)
    def _():
        await_bytes(rw, r_rw)
        total = rw[0].astype(F32)
        for k in range(1, 16):
            total += rw[k].astype(F32)
        gwf[...] = total.astype(BF16)
        row = pl.ds(pl.multiple_of(zl * 64, 64), 64)
        gather_send(gwf, gg.at[row], s_gw, r_gw)

    @pl.when(owner)
    def _():
        await_bytes(rz, r_c2)
        ct[...] = jnp.sum(rz[...], axis=0)
        pltpu.make_async_copy(ct, cvs.at[me], r_c3).start()

        def send(i, carry):
            remote(ct, cvs.at[me], s_c3, r_c3, plane(lax.rem(me + i, 32))).start()
            return carry

        lax.fori_loop(1, 32, send, 0)

    low = pl.ds(0, 512)
    high = pl.ds(512, 128)

    @pl.when(native)
    def _():
        for n in range(CHUNKS):
            part = pl.ds(n * W, W)
            await_bytes(gf_out.at[:, part], r_gf.at[n])
            remote(
                gf_out.at[:, part], gf_out.at[:, part], s_sib.at[n], r_gf.at[n], sibling
            ).start()
        await_bytes(gg.at[high], r_gb)
        remote(gg.at[high], gg.at[high], s_sib.at[CHUNKS], r_gb, sibling).start()
        await_bytes(gg.at[low], r_gw)
        remote(gg.at[low], gg.at[low], s_sib.at[CHUNKS + 1], r_gw, sibling).start()

    @pl.when(jnp.logical_not(native))
    def _():
        for n in range(CHUNKS):
            await_bytes(gf_out.at[:, pl.ds(n * W, W)], r_gf.at[n])
        await_bytes(gg.at[high], r_gb)
        await_bytes(gg.at[low], r_gw)

    outer = gg[low, :]
    inner = gg[high, :]
    a = iota((128, 512), 0)
    r = iota((128, 512), 1)
    of_block = (r // 16 == a // 4) & (lax.rem(r // 2, 4) == lax.rem(a, 4))
    for p in range(2):
        half = pl.ds(p * 128, 128)
        part_row = of_block & (lax.rem(r, 2) == p)
        pick = (part_row & (lax.rem(r // 8, 2) == 0)).astype(BF16)
        one_out[half, :] = dot(pick, outer).astype(BF16)
        pick = (part_row & (lax.rem(r // 8, 2) == 1)).astype(BF16)
        by_k = dot(pick, outer).astype(BF16)
        sign = jnp.where(iota((128, 128), 0) == iota((128, 128), 1), 1.0 - 2.0 * p, 0.0)
        four_out[half, :] = dot_nt(sign.astype(BF16), by_k).astype(BF16)
    for kk in range(4):
        pick = (iota((32, 128), 1) == 4 * iota((32, 128), 0) + kk).astype(BF16)
        by_j = dot(pick, inner).astype(BF16)
        turned = dot_nt(eye, by_j).astype(BF16)
        for ri in range(2):
            two_out[ri, kk] = turned[ri * 32 : (ri + 1) * 32]
            three_out[ri, kk] = by_j[:, 64 + ri * 32 : 96 + ri * 32]
    await_bytes(cvs, r_c3)
    for k in range(12):
        lanes = pl.ds(k * 128, 128)
        tapv_out[:, lanes] = cvs[k, pl.ds(0, 3), :]
        tapg_out[:, lanes] = cvs[k, pl.ds(3, 3), :]
    for n in range(CHUNKS):
        await_bytes(gx_out.at[:, pl.ds(n * W, W)], r_out.at[n])

    @pl.when(jnp.logical_not(native))
    def _():
        swap_left(0, 2)
        swap_left(2 * CHUNKS, 2 * CHUNKS + 2)
        for n in range(CHUNKS):
            await_bytes(gxs.at[:, pl.ds(n * W, W)], s_out.at[n])

        @pl.when((zl < 3) | (zl > 4))
        def _():
            await_bytes(fa, s_fa.at[0])
            await_bytes(fl, s_fa.at[1])

    @pl.when(me > 0)
    def _():
        await_bytes(halo.at[1], s_halo.at[0])
        for n in range(CHUNKS):
            await_bytes(es.at[0, :, pl.ds(n * W, W)], s_e.at[n, 0])

    @pl.when(me < 31)
    def _():
        await_bytes(halo.at[0], s_halo.at[1])
        for n in range(CHUNKS):
            await_bytes(es.at[1, :, pl.ds(n * W, W)], s_e.at[n, 1])

    for n in range(CHUNKS):
        part = pl.ds(n * W, W)
        await_bytes(xs.at[pl.ds(0, 31), :, part], s_x.at[n])
        await_bytes(zs.at[pl.ds(0, 31), :, part], s_z.at[n])

    @pl.when(native)
    def _():
        @pl.when((zl == 0) | (zl == 7))
        def _():
            await_bytes(fa, s_fa.at[0])
            await_bytes(fl, s_fa.at[1])

        for n in range(CHUNKS):
            part = pl.ds(n * W, W)
            await_bytes(ft.at[pl.ds(0, 112), part], s_rf.at[n])
            await_bytes(gf_out.at[pl.ds(0, 112), part], s_gf.at[n])
            await_bytes(gf_out.at[:, part], s_sib.at[n])
        await_bytes(gbs.at[pl.ds(0, 112)], s_rb)
        await_bytes(gws.at[pl.ds(0, 448)], s_rw)
        await_bytes(gbs.at[pl.ds(0, 112)], s_gb)
        await_bytes(gws.at[pl.ds(0, 448)], s_gw)
        await_bytes(gg.at[high], s_sib.at[CHUNKS])
        await_bytes(gg.at[low], s_sib.at[CHUNKS + 1])

    @pl.when(jnp.logical_not(native))
    def _():
        for n in range(CHUNKS):
            await_bytes(ft.at[:, pl.ds(n * W, W)], s_rf.at[n])
        await_bytes(gbs, s_rb)
        await_bytes(gws, s_rw)

    @pl.when(owner)
    def _():
        await_bytes(cp.at[pl.ds(0, 11)], s_c1)
        await_bytes(rz.at[pl.ds(0, 15)], s_c2)
        await_bytes(rc.at[pl.ds(0, 31)], s_c3)

    @pl.when(jnp.logical_not(owner))
    def _():
        await_bytes(cp, s_c1)


def mixer(tok, ups, flog, fact, cval, cgate):
    vmem = pl.BlockSpec(memory_space=pltpu.VMEM)
    hbm = pl.BlockSpec(memory_space=pl.ANY)
    dma = pltpu.SemaphoreType.DMA
    scratch = [
        ((640, 128), BF16),
        ((12, 8, 128), F32),
        ((128, C), BF16),
        ((128, C), BF16),
        ((128, C), BF16),
        ((1024, 128), BF16),
        ((2, 16, C), BF16),
        ((512, 256), BF16),
        ((256, 512), BF16),
        ((512, 512), BF16),
        ((512, 512), BF16),
        ((128, C), F32),
        ((256, C), BF16),
        ((32, 16, C), BF16),
        ((32, 16, C), BF16),
        ((512, C), BF16),
        ((32, 16, C), BF16),
        ((32, 16, C), BF16),
        ((128, C), BF16),
        ((128, 128), BF16),
        ((512, 128), BF16),
        ((512, 512), F32),
        ((512, 256), F32),
        ((128, C), F32),
        ((128, C), F32),
        ((2, 8, C), F32),
        ((2, 8, C), F32),
        ((128, C), BF16),
        ((16, 16, C), BF16),
        ((16, 16, 128), BF16),
        ((16, 64, 128), BF16),
        ((16, C), BF16),
        ((16, 128), BF16),
        ((64, 128), BF16),
        ((12, 8, 128), F32),
        ((32, 8, 128), F32),
        ((8, 128), F32),
        ((16, 8, 128), F32),
        ((8, 128), F32),
    ]
    n = CHUNKS
    sems = [
        (2 + 2 * n,),
        (),
        (n,),
        (n,),
        (2,),
        (2,),
        (2,),
        (2,),
        (n,),
        (n,),
        (n,),
        (n,),
        (n, 2),
        (n, 2),
        (n,),
        (n,),
        (n,),
        (n,),
        (),
        (),
        (),
        (),
        (n,),
        (n,),
        (),
        (),
        (),
        (),
        (n + 2,),
        (),
        (),
        (),
        (),
        (),
        (),
    ]
    return pl.pallas_call(
        kernel,
        out_shape=(
            jax.ShapeDtypeStruct((128, C), BF16),
            jax.ShapeDtypeStruct((128, C), BF16),
            jax.ShapeDtypeStruct((256, 128), BF16),
            jax.ShapeDtypeStruct((256, 128), BF16),
            jax.ShapeDtypeStruct((2, 4, 32, 32), BF16),
            jax.ShapeDtypeStruct((2, 4, 32, 32), BF16),
            jax.ShapeDtypeStruct((3, C), F32),
            jax.ShapeDtypeStruct((3, C), F32),
        ),
        in_specs=[hbm, hbm, hbm, hbm, vmem, vmem],
        out_specs=(vmem,) * 8,
        scratch_shapes=[pltpu.VMEM(shape, kind) for shape, kind in scratch]
        + [dma(shape) for shape in sems],
        compiler_params=pltpu.CompilerParams(
            collective_id=0, has_side_effects=True, vmem_limit_bytes=56 << 20
        ),
        name="mixer",
    )(tok, ups, flog, fact, cval, cgate)


def complex_stack(factor):
    real_part = factor[0]
    imag_part = factor[1]
    return jnp.stack([jnp.stack([real_part, -imag_part]), jnp.stack([imag_part, real_part])])


def shards(
    tokens, upstream, conv_value, conv_gate, mix_one, mix_two, mix_three, mix_four, filter_log
):
    one = mix_one[:, 0].transpose(1, 0, 2).reshape(32, 1, 8, 128)
    signed = jnp.stack([mix_four[0, 0], -mix_four[1, 0]])
    four = signed.transpose(2, 0, 1).reshape(32, 1, 8, 128)
    wide = jnp.concatenate([one, four], axis=1).reshape(512, 128)
    two = complex_stack(mix_two).transpose(4, 2, 1, 0, 3).reshape(32, 1, 8, 64)
    three = complex_stack(mix_three).transpose(3, 2, 0, 1, 4).reshape(32, 1, 8, 64)
    narrow = jnp.concatenate([two, three], axis=1).reshape(512, 64)
    factors = jnp.concatenate([wide, jnp.pad(narrow, ((0, 0), (0, 64)))], axis=0)
    grad_x, grad_filter, grad_one, grad_four, grad_two, grad_three, taps, gates = mixer(
        tokens[0],
        upstream[0],
        filter_log.reshape(128, C),
        factors,
        conv_value,
        conv_gate,
    )
    return (
        grad_x[None],
        taps,
        gates,
        grad_one.reshape(2, 1, 128, 128),
        grad_two,
        grad_three,
        grad_four.reshape(2, 1, 128, 128),
        grad_filter.reshape(4, 32, C),
    )


def solution(mesh):
    inner = Mesh(mesh.devices.reshape(8, 2, 2, 16), ALL)
    rows = ("zl", "co")
    cols = ("zh", "xy")
    block = P(None, cols, None, None)
    return jax.shard_map(
        shards,
        mesh=inner,
        in_specs=(
            P(rows, cols, None),
            P(rows, cols, None),
            P(),
            P(),
            block,
            block,
            block,
            block,
            P(cols, None, None),
        ),
        out_specs=(
            P(rows, cols, None),
            P(),
            P(),
            block,
            block,
            block,
            block,
            P(cols, None, None),
        ),
        check_vma=False,
    )
```

```python
import jax
import jax.numpy as jnp
from jax import lax
from jax.experimental import pallas as pl
from jax.experimental.pallas import tpu as pltpu
from jax.sharding import Mesh, PartitionSpec as P

C = 1536
ALL = ("zl", "co", "zh", "xy")
MESH = pl.DeviceIdType.MESH
F32 = jnp.float32
BF16 = jnp.bfloat16
CHUNKS = 2
W = C // CHUNKS
TILE = 256
TILES = W // TILE


def iota(shape, dim):
    return lax.broadcasted_iota(jnp.int32, shape, dim)


def dot(a, b):
    return lax.dot_general(a, b, (((1,), (0,)), ((), ())), preferred_element_type=F32)


def dot_nt(a, b):
    return lax.dot_general(a, b, (((1,), (1,)), ((), ())), preferred_element_type=F32)


def await_bytes(ref, sem):
    pltpu.make_async_copy(ref, ref, sem).wait()


def kernel(
    tok,
    ups,
    flog,
    fact,
    cval,
    cgate,
    gx_out,
    gf_out,
    one_out,
    four_out,
    two_out,
    three_out,
    tapv_out,
    tapg_out,
    gg,
    cvs,
    ts,
    us,
    fl,
    fa,
    halo,
    w14,
    w14t,
    bmat,
    bmatt,
    filt,
    ymat,
    xs,
    xr,
    vmat,
    zs,
    zr,
    ft,
    gbs,
    gws,
    dbm,
    dwm,
    vgs,
    ggs,
    es,
    er,
    gxs,
    rf,
    rb,
    rw,
    fin,
    gbf,
    gwf,
    cp,
    rc,
    cs,
    rz,
    ct,
    s_in,
    r_edge,
    r_t,
    r_u,
    s_fa,
    r_fa,
    s_halo,
    r_halo,
    s_x,
    r_x,
    s_z,
    r_z,
    s_e,
    r_e,
    s_out,
    r_out,
    s_rf,
    r_rf,
    s_rb,
    r_rb,
    s_rw,
    r_rw,
    s_gf,
    r_gf,
    s_gb,
    r_gb,
    s_gw,
    r_gw,
    s_sib,
    s_c1,
    r_c1,
    s_c2,
    r_c2,
    s_c3,
    r_c3,
):
    zl, co, zh, xy = (lax.axis_index(name) for name in ALL)
    me = co * 16 + xy
    z = zh * 8 + zl
    native = co == zh
    partner = (zl, 1 - co, 1 - zh, xy)
    sibling = (zl, 1 - co, zh, xy)

    def plane(j):
        return (zl, j // 16, zh, lax.rem(j, 16))

    def ring(k):
        return (lax.rem(k, 8), co, k // 8, xy)

    def remote(src, dst, ss, rs, dev):
        return pltpu.make_async_remote_copy(
            src_ref=src, dst_ref=dst, send_sem=ss, recv_sem=rs, device_id=dev, device_id_type=MESH
        )

    up = lax.rem(z + 1, 16)
    down = lax.rem(z + 15, 16)

    barrier = pltpu.get_barrier_semaphore()

    def greet_plane(i, carry):
        pl.semaphore_signal(
            barrier, inc=1, device_id=plane(lax.rem(me + i, 32)), device_id_type=MESH
        )
        return carry

    def greet_ring(i, carry):
        pl.semaphore_signal(
            barrier, inc=1, device_id=ring(lax.rem(z + i, 16)), device_id_type=MESH
        )
        return carry

    pl.semaphore_signal(barrier, inc=1, device_id=partner, device_id_type=MESH)
    lax.fori_loop(1, 16, greet_ring, 0)
    lax.fori_loop(1, 32, greet_plane, 0)
    pl.semaphore_wait(barrier, 47)

    def role_copies():
        out = []
        for lo, hi in ((0, 16), (112, 128)):
            part = pl.ds(lo, hi - lo)
            out.append((tok.at[part], ts.at[part], r_edge))
        for n in range(CHUNKS):
            cols = pl.ds(n * W, W)
            mid = pl.ds(16, 96)
            out.append((tok.at[mid, cols], ts.at[mid, cols], r_t.at[n]))
            out.append((ups.at[:, cols], us.at[:, cols], r_u.at[n]))
        return out

    @pl.when(native)
    def _():
        pltpu.make_async_copy(fact, fa, r_fa.at[0]).start()
        pltpu.make_async_copy(flog, fl, r_fa.at[1]).start()
        for src, dst, sem in role_copies():
            pltpu.make_async_copy(src, dst, sem).start()

        @pl.when(zl == 0)
        def _():
            remote(fact, fa, s_fa.at[0], r_fa.at[0], ring(down)).start()
            remote(flog, fl, s_fa.at[1], r_fa.at[1], ring(down)).start()

        @pl.when(zl == 7)
        def _():
            remote(fact, fa, s_fa.at[0], r_fa.at[0], ring(up)).start()
            remote(flog, fl, s_fa.at[1], r_fa.at[1], ring(up)).start()

    def swap_in(lo, hi):
        for i, (src, dst, sem) in enumerate(role_copies()):
            if lo <= i < hi:
                remote(src, dst, s_in.at[i], sem, partner).start()

    def swap_left(lo, hi):
        for i, (src, dst, sem) in enumerate(role_copies()):
            if lo <= i < hi:
                await_bytes(dst, s_in.at[i])

    @pl.when(jnp.logical_not(native))
    def _():
        swap_in(0, 2 * CHUNKS + 2)

    def forward(src, slot):
        @pl.when(jnp.logical_not(native) & (zl < 3))
        def _():
            remote(src, src, s_fa.at[slot], r_fa.at[slot], ring(up)).start()

        @pl.when(jnp.logical_not(native) & (zl > 4))
        def _():
            remote(src, src, s_fa.at[slot], r_fa.at[slot], ring(down)).start()

    await_bytes(ts.at[pl.ds(0, 32)], r_edge)

    @pl.when(me > 0)
    def _():
        remote(ts.at[pl.ds(0, 16)], halo.at[1], s_halo.at[0], r_halo.at[1], plane(me - 1)).start()

    @pl.when(me < 31)
    def _():
        remote(
            ts.at[pl.ds(112, 16)], halo.at[0], s_halo.at[1], r_halo.at[0], plane(me + 1)
        ).start()

    await_bytes(fa, r_fa.at[0])
    forward(fa, 0)
    wc = fa[pl.ds(0, 512), :]
    first_row = lax.rem(iota((512, 128), 0) // 8, 2) == 0
    zero = jnp.zeros_like(wc)
    w14[:, pl.ds(0, 128)] = jnp.where(first_row, wc, zero)
    w14[:, pl.ds(128, 128)] = jnp.where(first_row, zero, wc)
    eye = (iota((128, 128), 0) == iota((128, 128), 1)).astype(BF16)
    wct = dot_nt(eye, wc)
    first_col = lax.rem(iota((128, 512), 1) // 8, 2) == 0
    w14t[pl.ds(0, 128), :] = jnp.where(first_col, wct, 0.0).astype(BF16)
    w14t[pl.ds(128, 128), :] = jnp.where(first_col, 0.0, wct).astype(BF16)

    def block_mask(rows, cols):
        return (lax.rem(rows // 8, 2) == cols // 256) & (
            lax.rem(rows // 2, 4) == lax.rem(cols // 32, 4)
        )

    dc = fa[pl.ds(512, 512), :]
    for n in range(4):
        part = pl.ds(n * 128, 128)
        s = iota((128, 128), 1) + n * 128
        l = iota((128, 128), 0)
        spread = (l == lax.rem(s // 128, 2) * 32 + lax.rem(s, 32)).astype(BF16)
        wide = dot(dc, spread)
        keep = block_mask(iota((512, 128), 0), iota((512, 128), 1) + n * 128)
        bmat[:, part] = jnp.where(keep, wide, 0.0).astype(BF16)
        s = iota((128, 128), 0) + n * 128
        l = iota((128, 128), 1)
        spread = (l == lax.rem(s // 128, 2) * 32 + lax.rem(s, 32)).astype(BF16)
        tall = dot_nt(spread, dc)
        keep = block_mask(iota((128, 512), 1), iota((128, 512), 0) + n * 128)
        bmatt[part, :] = jnp.where(keep, tall, 0.0).astype(BF16)

    dbm[...] = jnp.zeros_like(dbm)
    dwm[...] = jnp.zeros_like(dwm)

    @pl.when(me == 0)
    def _():
        halo[0] = jnp.zeros((16, C), BF16)

    @pl.when(me == 31)
    def _():
        halo[1] = jnp.zeros((16, C), BF16)

    @pl.when(me > 0)
    def _():
        await_bytes(halo.at[0], r_halo.at[0])

    @pl.when(me < 31)
    def _():
        await_bytes(halo.at[1], r_halo.at[1])

    rows = iota((128, TILE), 0)

    def shifted(x, before, after):
        prev = jnp.where(rows == 0, before, pltpu.roll(x, 1, axis=0))
        nxt = jnp.where(rows == 127, after, pltpu.roll(x, 127, axis=0))
        return prev, nxt

    def token_windows(cols):
        x = ts[:, cols].astype(F32)
        before = halo[0, :, cols].astype(F32)[15:16]
        after = halo[1, :, cols].astype(F32)[0:1]
        prev, nxt = shifted(x, before, after)
        return prev, x, nxt

    def tile_cols(n, i):
        return pl.ds(pl.multiple_of(n * W + i * TILE, TILE), TILE)

    def all_to_all(src, dst, ss, rs, n):
        cols = pl.ds(n * W, W)

        def send(i, carry):
            j = lax.rem(me + i, 32)
            remote(src.at[j, :, cols], dst.at[me, :, cols], ss.at[n], rs.at[n], plane(j)).start()
            return carry

        lax.fori_loop(1, 32, send, 0)
        pltpu.make_async_copy(src.at[me, :, cols], dst.at[me, :, cols], rs.at[n]).start()

    def phase_one(n):
        part = pl.ds(n * W, W)
        await_bytes(ts.at[pl.ds(16, 96), part], r_t.at[n])
        await_bytes(us.at[:, part], r_u.at[n])

        def tile(i, carry):
            cols = tile_cols(n, i)
            prev, x, nxt = token_windows(cols)
            cv = cval[:, cols]
            cg = cgate[:, cols]
            values = cv[0:1] * prev + cv[1:2] * x + cv[2:3] * nxt
            gating = (cg[0:1] * prev + cg[1:2] * x + cg[2:3] * nxt).astype(BF16).astype(F32)
            mix = us[:, cols].astype(F32) * gating
            ymat[pl.ds(0, 128), cols] = values.astype(BF16)
            ymat[pl.ds(128, 128), cols] = mix.astype(BF16)
            y = ymat[:, cols]
            xs[:, :, cols] = dot(w14[...], y).astype(BF16).reshape(32, 16, TILE)
            return carry

        lax.fori_loop(0, TILES, tile, 0)
        all_to_all(xs, xr, s_x, r_x, n)

    def reduce_send(src, size, dst, ss, rs):
        def send(k, carry):
            piece = src(pl.ds(pl.multiple_of(k * size, size), size))
            mine = native & (k == zl)

            @pl.when(mine)
            def _():
                pltpu.make_async_copy(piece, dst, rs).start()

            @pl.when(jnp.logical_not(mine))
            def _():
                remote(piece, dst, ss, rs, (k, co, co, xy)).start()

            return carry

        lax.fori_loop(0, 8, send, 0)

    def gather_send(src, dst, ss, rs):
        pltpu.make_async_copy(src, dst, rs).start()

        def send(i, carry):
            k = lax.rem(zl + i, 8)
            remote(src, dst, ss, rs, (k, co, co, xy)).start()
            return carry

        lax.fori_loop(1, 8, send, 0)

    def phase_two(n):
        part = pl.ds(n * W, W)
        await_bytes(xr.at[:, :, part], r_x.at[n])

        def tile(i, carry):
            cols = tile_cols(n, i)
            x = xr[:, :, cols].reshape(512, TILE)
            both = dot(bmatt[...], x)
            f = jnp.exp(fl[:, cols].astype(F32))
            filt[:, cols] = f
            sr = both[0:128]
            si = both[128:256]
            gr = both[256:384]
            gi = both[384:512]
            ft[:, cols] = (gr * sr + gi * si).astype(BF16)
            vmat[pl.ds(0, 128), cols] = (f * gr).astype(BF16)
            vmat[pl.ds(128, 128), cols] = (f * gi).astype(BF16)
            vmat[pl.ds(256, 128), cols] = (f * sr).astype(BF16)
            vmat[pl.ds(384, 128), cols] = (f * si).astype(BF16)
            v = vmat[:, cols]
            zs[:, :, cols] = dot(bmat[...], v).astype(BF16).reshape(32, 16, TILE)
            return carry

        lax.fori_loop(0, TILES, tile, 0)
        all_to_all(zs, zr, s_z, r_z, n)
        reduce_send(lambda piece: ft.at[piece, part], 16, rf.at[z, :, part], s_rf.at[n], r_rf.at[n])

        def tile_grad(i, carry):
            cols = tile_cols(n, i)
            dbm[...] += dot_nt(xr[:, :, cols].reshape(512, TILE), vmat[:, cols])
            return carry

        lax.fori_loop(0, TILES, tile_grad, 0)

    def phase_three(n):
        part = pl.ds(n * W, W)
        await_bytes(zr.at[:, :, part], r_z.at[n])

        def tile(i, carry):
            cols = tile_cols(n, i)
            zt = zr[:, :, cols].reshape(512, TILE)
            both = dot(w14t[...], zt)
            vg = both[0:128]
            gg = us[:, cols].astype(F32) * both[128:256]
            vgs[:, cols] = vg
            ggs[:, cols] = gg
            cv = cval[:, cols]
            cg = cgate[:, cols]
            es[0, :, cols] = jnp.broadcast_to(cv[0:1] * vg[0:1] + cg[0:1] * gg[0:1], (8, TILE))
            es[1, :, cols] = jnp.broadcast_to(
                cv[2:3] * vg[127:128] + cg[2:3] * gg[127:128], (8, TILE)
            )
            return carry

        lax.fori_loop(0, TILES, tile, 0)

        @pl.when(me > 0)
        def _():
            remote(
                es.at[0, :, part], er.at[1, :, part], s_e.at[n, 0], r_e.at[n, 1], plane(me - 1)
            ).start()

        @pl.when(me < 31)
        def _():
            remote(
                es.at[1, :, part], er.at[0, :, part], s_e.at[n, 1], r_e.at[n, 0], plane(me + 1)
            ).start()

        def tile_grad(i, carry):
            cols = tile_cols(n, i)
            prev, x, nxt = token_windows(cols)
            row = lax.broadcasted_iota(jnp.int32, (8, TILE), 0)
            total = jnp.zeros((8, TILE), F32)
            for at, grad in ((0, vgs[:, cols]), (3, ggs[:, cols])):
                for o, window in enumerate((prev, x, nxt)):
                    total += jnp.where(
                        row == at + o, jnp.sum(grad * window, axis=0, keepdims=True), 0.0
                    )
            for k in range(TILE // 128):
                cp[(n * W + i * TILE) // 128 + k] = total[:, k * 128 : (k + 1) * 128]
            dwm[...] += dot_nt(zr[:, :, cols].reshape(512, TILE), ymat[:, cols])
            return carry

        lax.fori_loop(0, TILES, tile_grad, 0)

    def phase_out(n):
        part = pl.ds(n * W, W)

        @pl.when(me == 0)
        def _():
            er[0, :, part] = jnp.zeros((8, W), F32)

        @pl.when(me == 31)
        def _():
            er[1, :, part] = jnp.zeros((8, W), F32)

        @pl.when(me > 0)
        def _():
            await_bytes(er.at[0, :, part], r_e.at[n, 0])

        @pl.when(me < 31)
        def _():
            await_bytes(er.at[1, :, part], r_e.at[n, 1])

        def tile(i, carry):
            cols = tile_cols(n, i)
            cv = cval[:, cols]
            cg = cgate[:, cols]
            vg = vgs[:, cols]
            gg = ggs[:, cols]
            ahead = cv[0:1] * vg + cg[0:1] * gg
            behind = cv[2:3] * vg + cg[2:3] * gg
            here = cv[1:2] * vg + cg[1:2] * gg
            first = er[0, :, cols][0:1]
            last = er[1, :, cols][0:1]
            down_rows = jnp.where(rows == 0, first, pltpu.roll(behind, 1, axis=0))
            up_rows = jnp.where(rows == 127, last, pltpu.roll(ahead, 127, axis=0))
            gxs[:, cols] = (up_rows + here + down_rows).astype(BF16)
            return carry

        lax.fori_loop(0, TILES, tile, 0)

        @pl.when(native)
        def _():
            pltpu.make_async_copy(gxs.at[:, part], gx_out.at[:, part], r_out.at[n]).start()

        @pl.when(jnp.logical_not(native))
        def _():
            remote(
                gxs.at[:, part], gx_out.at[:, part], s_out.at[n], r_out.at[n], partner
            ).start()

    def filter_finish(n):
        part = pl.ds(n * W, W)

        @pl.when(native)
        def _():
            await_bytes(rf.at[:, :, part], r_rf.at[n])

            def tile(i, carry):
                cols = tile_cols(n, i)
                total = rf[0, :, cols].astype(F32)
                for k in range(1, 16):
                    total += rf[k, :, cols].astype(F32)
                share = filt[pl.ds(pl.multiple_of(zl * 16, 16), 16), cols]
                fin[:, cols] = (share * total).astype(BF16)
                return carry

            lax.fori_loop(0, TILES, tile, 0)
            mine = pl.ds(pl.multiple_of(zl * 16, 16), 16)
            gather_send(fin.at[:, part], gf_out.at[mine, part], s_gf.at[n], r_gf.at[n])

    def inner_grads():
        keep_rows = iota((512, 128), 0)
        packed = [jnp.zeros((512, 128), F32), jnp.zeros((512, 128), F32)]
        for n in range(4):
            part = pl.ds(n * 128, 128)
            keep = block_mask(keep_rows, iota((512, 128), 1) + n * 128)
            q = jnp.where(keep, dbm[:, part], 0.0).astype(BF16)
            s = iota((128, 128), 0) + n * 128
            l = iota((128, 128), 1)
            same = (s // 256 == l // 64) & (lax.rem(s, 32) == lax.rem(l, 32))
            part_of = lax.rem(s // 128, 2)
            imag = lax.rem(l // 32, 2)
            for p in range(2):
                hit = same & (part_of == (imag if p == 0 else 1 - imag))
                minus = (imag == 1) & (l // 64 != p)
                sel = jnp.where(hit, jnp.where(minus, -1.0, 1.0), 0.0).astype(BF16)
                packed[p] = packed[p] + dot(q, sel)
        gb = jnp.zeros((128, 128), F32)
        a = iota((128, 512), 0)
        r = iota((128, 512), 1)
        for p in range(2):
            pick = (r // 16 == a // 4) & (lax.rem(r // 2, 4) == lax.rem(a, 4)) & (lax.rem(r, 2) == p)
            gb = gb + dot(pick.astype(BF16), packed[p].astype(BF16))
        gbs[...] = gb.astype(BF16)
        reduce_send(lambda piece: gbs.at[piece], 16, rb.at[z], s_rb, r_rb)

    def filter_in():
        await_bytes(fl, r_fa.at[1])
        forward(fl, 1)

    for n in range(CHUNKS):
        phase_one(n)
    filter_in()
    for n in range(CHUNKS):
        phase_two(n)
    inner_grads()
    for n in range(CHUNKS):
        phase_three(n)
        phase_out(n)
    for n in range(CHUNKS):
        filter_finish(n)

    t_first = lax.rem(iota((512, 128), 0) // 8, 2) == 0
    gws[...] = jnp.where(t_first, dwm[:, pl.ds(0, 128)], dwm[:, pl.ds(128, 128)]).astype(BF16)
    reduce_send(lambda piece: gws.at[piece], 64, rw.at[z], s_rw, r_rw)

    def tap_send(k, carry):
        @pl.when(k == me)
        def _():
            pltpu.make_async_copy(cp.at[k], rc.at[me], r_c1).start()

        @pl.when(k != me)
        def _():
            remote(cp.at[k], rc.at[me], s_c1, r_c1, plane(k)).start()

        return carry

    lax.fori_loop(0, 12, tap_send, 0)

    @pl.when(native)
    def _():
        await_bytes(rb, r_rb)
        total = rb[0].astype(F32)
        for k in range(1, 16):
            total += rb[k].astype(F32)
        gbf[...] = total.astype(BF16)
        row = pl.ds(pl.multiple_of(512 + zl * 16, 16), 16)
        gather_send(gbf, gg.at[row], s_gb, r_gb)

    owner = me < 12

    @pl.when(owner)
    def _():
        await_bytes(rc, r_c1)
        cs[...] = jnp.sum(rc[...], axis=0)
        pltpu.make_async_copy(cs, rz.at[z], r_c2).start()

        def send(i, carry):
            remote(cs, rz.at[z], s_c2, r_c2, ring(lax.rem(z + i, 16))).start()
            return carry

        lax.fori_loop(1, 16, send, 0)

    @pl.when(native)
    def _():
        await_bytes(rw, r_rw)
        total = rw[0].astype(F32)
        for k in range(1, 16):
            total += rw[k].astype(F32)
        gwf[...] = total.astype(BF16)
        row = pl.ds(pl.multiple_of(zl * 64, 64), 64)
        gather_send(gwf, gg.at[row], s_gw, r_gw)

    @pl.when(owner)
    def _():
        await_bytes(rz, r_c2)
        ct[...] = jnp.sum(rz[...], axis=0)
        pltpu.make_async_copy(ct, cvs.at[me], r_c3).start()

        def send(i, carry):
            remote(ct, cvs.at[me], s_c3, r_c3, plane(lax.rem(me + i, 32))).start()
            return carry

        lax.fori_loop(1, 32, send, 0)

    low = pl.ds(0, 512)
    high = pl.ds(512, 128)

    @pl.when(native)
    def _():
        for n in range(CHUNKS):
            part = pl.ds(n * W, W)
            await_bytes(gf_out.at[:, part], r_gf.at[n])
            remote(
                gf_out.at[:, part], gf_out.at[:, part], s_sib.at[n], r_gf.at[n], sibling
            ).start()
        await_bytes(gg.at[high], r_gb)
        remote(gg.at[high], gg.at[high], s_sib.at[CHUNKS], r_gb, sibling).start()
        await_bytes(gg.at[low], r_gw)
        remote(gg.at[low], gg.at[low], s_sib.at[CHUNKS + 1], r_gw, sibling).start()

    @pl.when(jnp.logical_not(native))
    def _():
        for n in range(CHUNKS):
            await_bytes(gf_out.at[:, pl.ds(n * W, W)], r_gf.at[n])
        await_bytes(gg.at[high], r_gb)
        await_bytes(gg.at[low], r_gw)

    outer = gg[low, :]
    inner = gg[high, :]
    a = iota((128, 512), 0)
    r = iota((128, 512), 1)
    of_block = (r // 16 == a // 4) & (lax.rem(r // 2, 4) == lax.rem(a, 4))
    for p in range(2):
        half = pl.ds(p * 128, 128)
        part_row = of_block & (lax.rem(r, 2) == p)
        pick = (part_row & (lax.rem(r // 8, 2) == 0)).astype(BF16)
        one_out[half, :] = dot(pick, outer).astype(BF16)
        pick = (part_row & (lax.rem(r // 8, 2) == 1)).astype(BF16)
        by_k = dot(pick, outer).astype(BF16)
        sign = jnp.where(iota((128, 128), 0) == iota((128, 128), 1), 1.0 - 2.0 * p, 0.0)
        four_out[half, :] = dot_nt(sign.astype(BF16), by_k).astype(BF16)
    for kk in range(4):
        pick = (iota((32, 128), 1) == 4 * iota((32, 128), 0) + kk).astype(BF16)
        by_j = dot(pick, inner).astype(BF16)
        turned = dot_nt(eye, by_j).astype(BF16)
        for ri in range(2):
            two_out[ri, kk] = turned[ri * 32 : (ri + 1) * 32]
            three_out[ri, kk] = by_j[:, 64 + ri * 32 : 96 + ri * 32]
    await_bytes(cvs, r_c3)
    for k in range(12):
        lanes = pl.ds(k * 128, 128)
        tapv_out[:, lanes] = cvs[k, pl.ds(0, 3), :]
        tapg_out[:, lanes] = cvs[k, pl.ds(3, 3), :]
    for n in range(CHUNKS):
        await_bytes(gx_out.at[:, pl.ds(n * W, W)], r_out.at[n])

    @pl.when(jnp.logical_not(native))
    def _():
        swap_left(0, 2 * CHUNKS + 2)
        for n in range(CHUNKS):
            await_bytes(gxs.at[:, pl.ds(n * W, W)], s_out.at[n])

        @pl.when((zl < 3) | (zl > 4))
        def _():
            await_bytes(fa, s_fa.at[0])
            await_bytes(fl, s_fa.at[1])

    @pl.when(me > 0)
    def _():
        await_bytes(halo.at[1], s_halo.at[0])
        for n in range(CHUNKS):
            await_bytes(es.at[0, :, pl.ds(n * W, W)], s_e.at[n, 0])

    @pl.when(me < 31)
    def _():
        await_bytes(halo.at[0], s_halo.at[1])
        for n in range(CHUNKS):
            await_bytes(es.at[1, :, pl.ds(n * W, W)], s_e.at[n, 1])

    for n in range(CHUNKS):
        part = pl.ds(n * W, W)
        await_bytes(xs.at[pl.ds(0, 31), :, part], s_x.at[n])
        await_bytes(zs.at[pl.ds(0, 31), :, part], s_z.at[n])

    @pl.when(native)
    def _():
        @pl.when((zl == 0) | (zl == 7))
        def _():
            await_bytes(fa, s_fa.at[0])
            await_bytes(fl, s_fa.at[1])

        for n in range(CHUNKS):
            part = pl.ds(n * W, W)
            await_bytes(ft.at[pl.ds(0, 112), part], s_rf.at[n])
            await_bytes(gf_out.at[pl.ds(0, 112), part], s_gf.at[n])
            await_bytes(gf_out.at[:, part], s_sib.at[n])
        await_bytes(gbs.at[pl.ds(0, 112)], s_rb)
        await_bytes(gws.at[pl.ds(0, 448)], s_rw)
        await_bytes(gbs.at[pl.ds(0, 112)], s_gb)
        await_bytes(gws.at[pl.ds(0, 448)], s_gw)
        await_bytes(gg.at[high], s_sib.at[CHUNKS])
        await_bytes(gg.at[low], s_sib.at[CHUNKS + 1])

    @pl.when(jnp.logical_not(native))
    def _():
        for n in range(CHUNKS):
            await_bytes(ft.at[:, pl.ds(n * W, W)], s_rf.at[n])
        await_bytes(gbs, s_rb)
        await_bytes(gws, s_rw)

    @pl.when(owner)
    def _():
        await_bytes(cp.at[pl.ds(0, 11)], s_c1)
        await_bytes(rz.at[pl.ds(0, 15)], s_c2)
        await_bytes(rc.at[pl.ds(0, 31)], s_c3)

    @pl.when(jnp.logical_not(owner))
    def _():
        await_bytes(cp, s_c1)


def mixer(tok, ups, flog, fact, cval, cgate):
    vmem = pl.BlockSpec(memory_space=pltpu.VMEM)
    hbm = pl.BlockSpec(memory_space=pl.ANY)
    dma = pltpu.SemaphoreType.DMA
    scratch = [
        ((640, 128), BF16),
        ((12, 8, 128), F32),
        ((128, C), BF16),
        ((128, C), BF16),
        ((128, C), BF16),
        ((1024, 128), BF16),
        ((2, 16, C), BF16),
        ((512, 256), BF16),
        ((256, 512), BF16),
        ((512, 512), BF16),
        ((512, 512), BF16),
        ((128, C), F32),
        ((256, C), BF16),
        ((32, 16, C), BF16),
        ((32, 16, C), BF16),
        ((512, C), BF16),
        ((32, 16, C), BF16),
        ((32, 16, C), BF16),
        ((128, C), BF16),
        ((128, 128), BF16),
        ((512, 128), BF16),
        ((512, 512), F32),
        ((512, 256), F32),
        ((128, C), F32),
        ((128, C), F32),
        ((2, 8, C), F32),
        ((2, 8, C), F32),
        ((128, C), BF16),
        ((16, 16, C), BF16),
        ((16, 16, 128), BF16),
        ((16, 64, 128), BF16),
        ((16, C), BF16),
        ((16, 128), BF16),
        ((64, 128), BF16),
        ((12, 8, 128), F32),
        ((32, 8, 128), F32),
        ((8, 128), F32),
        ((16, 8, 128), F32),
        ((8, 128), F32),
    ]
    n = CHUNKS
    sems = [
        (2 + 2 * n,),
        (),
        (n,),
        (n,),
        (2,),
        (2,),
        (2,),
        (2,),
        (n,),
        (n,),
        (n,),
        (n,),
        (n, 2),
        (n, 2),
        (n,),
        (n,),
        (n,),
        (n,),
        (),
        (),
        (),
        (),
        (n,),
        (n,),
        (),
        (),
        (),
        (),
        (n + 2,),
        (),
        (),
        (),
        (),
        (),
        (),
    ]
    return pl.pallas_call(
        kernel,
        out_shape=(
            jax.ShapeDtypeStruct((128, C), BF16),
            jax.ShapeDtypeStruct((128, C), BF16),
            jax.ShapeDtypeStruct((256, 128), BF16),
            jax.ShapeDtypeStruct((256, 128), BF16),
            jax.ShapeDtypeStruct((2, 4, 32, 32), BF16),
            jax.ShapeDtypeStruct((2, 4, 32, 32), BF16),
            jax.ShapeDtypeStruct((3, C), F32),
            jax.ShapeDtypeStruct((3, C), F32),
        ),
        in_specs=[hbm, hbm, hbm, hbm, vmem, vmem],
        out_specs=(vmem,) * 8,
        scratch_shapes=[pltpu.VMEM(shape, kind) for shape, kind in scratch]
        + [dma(shape) for shape in sems],
        compiler_params=pltpu.CompilerParams(
            collective_id=0, has_side_effects=True, vmem_limit_bytes=56 << 20
        ),
        name="mixer",
    )(tok, ups, flog, fact, cval, cgate)


def complex_stack(factor):
    real_part = factor[0]
    imag_part = factor[1]
    return jnp.stack([jnp.stack([real_part, -imag_part]), jnp.stack([imag_part, real_part])])


def shards(
    tokens, upstream, conv_value, conv_gate, mix_one, mix_two, mix_three, mix_four, filter_log
):
    one = mix_one[:, 0].transpose(1, 0, 2).reshape(32, 1, 8, 128)
    signed = jnp.stack([mix_four[0, 0], -mix_four[1, 0]])
    four = signed.transpose(2, 0, 1).reshape(32, 1, 8, 128)
    wide = jnp.concatenate([one, four], axis=1).reshape(512, 128)
    two = complex_stack(mix_two).transpose(4, 2, 1, 0, 3).reshape(32, 1, 8, 64)
    three = complex_stack(mix_three).transpose(3, 2, 0, 1, 4).reshape(32, 1, 8, 64)
    narrow = jnp.concatenate([two, three], axis=1).reshape(512, 64)
    factors = jnp.concatenate([wide, jnp.pad(narrow, ((0, 0), (0, 64)))], axis=0)
    grad_x, grad_filter, grad_one, grad_four, grad_two, grad_three, taps, gates = mixer(
        tokens[0],
        upstream[0],
        filter_log.reshape(128, C),
        factors,
        conv_value,
        conv_gate,
    )
    return (
        grad_x[None],
        taps,
        gates,
        grad_one.reshape(2, 1, 128, 128),
        grad_two,
        grad_three,
        grad_four.reshape(2, 1, 128, 128),
        grad_filter.reshape(4, 32, C),
    )


def solution(mesh):
    inner = Mesh(mesh.devices.reshape(8, 2, 2, 16), ALL)
    rows = ("zl", "co")
    cols = ("zh", "xy")
    block = P(None, cols, None, None)
    return jax.shard_map(
        shards,
        mesh=inner,
        in_specs=(
            P(rows, cols, None),
            P(rows, cols, None),
            P(),
            P(),
            block,
            block,
            block,
            block,
            P(cols, None, None),
        ),
        out_specs=(
            P(rows, cols, None),
            P(),
            P(),
            block,
            block,
            block,
            block,
            P(cols, None, None),
        ),
        check_vma=False,
    )
```
